32 devices in a mesh: beam: 2 (over x), chan: 8 (over z, y), tm: 2 (over core).
Axes of the slice: x: 2, y: 2, z: 4, core: 2. Of those that a mesh axis runs over, the one named last changes fastest.
Arguments:
- filterbank: bfloat16 [4096, 4096], P(('beam', 'chan'), 'tm'), parts along dimension 0, may hold values from -2500 to 2500
- local_delays: int32 [2048, 64], P('chan'), may hold values from 0 to 63
- lower_rows: int32 [3, 512], P(None, 'chan'), may hold values from 0 to 63
- upper_rows: int32 [3, 512], P(None, 'chan'), may hold values from 0 to 63
- level_shifts: int32 [3, 512], P(None, 'chan'), may hold values from 0 to 127, as said below
- box_widths: int32 [8], replicated, may hold values from 1 to 128, as said below
Outputs:
- snr: float32 [8, 1024, 4096], P(None, ('beam', 'chan'), 'tm'), parts along dimension 1
The draws below stay inside these ranges and needn't reach their ends.
There are 2 independent parts, one for each index of `beam`. The reference program is written for one: setup_inputs(seed, part) draws one part's arguments, and reference() takes and returns one part's arrays. A program takes and returns all parts, laid end to end along the dimension named above; an argument that names none is the same for every part. Nothing has to cross between parts.
Inputs may be any that keep to these rules, and one draw needn't show every extreme that they name: `level_shifts`: at level j every entry is below 64 * 2**j // 2, and that bound less one occurs at every level. `box_widths`: entry i lies in [2**i, 2**(i+1)) for i below 7; the last entry is 128.
All inputs are finite; a program needn't handle non-finite values.
Results may differ from the reference program's by a relative error of at most 0.0014.
Values may be sent and summed in bfloat16 or wider, within the bound.
A program may use at most 64 MiB of HBM per device.

```python
import math
import jax
import jax.numpy as jnp
from jax import lax

CH_DEV = 256
K = 64
DLOC = 64
NW = 8
XLEV = 3
WMAX = 128
CH = 2048
DMS = 512
TT = 4096
N_CHAN = 8


def draw_filterbank(key, part):
    key_gain = jax.random.fold_in(key, 11)
    key_noise = jax.random.fold_in(key, 12)
    moments = jnp.arange(TT, dtype=jnp.float32) / TT
    gains = jnp.exp(jax.random.uniform(key_gain, (CH, 1), minval=0.0, maxval=math.log(10.0)))
    envelope = jnp.exp(math.log(10.0) * moments)[None, :]
    noise = jnp.clip(jax.random.normal(key_noise, (CH, TT)), -6.0, 6.0)
    values = gains * envelope * noise
    return values.astype(jnp.bfloat16)


def draw_local_delays(key, part):
    key_values = jax.random.fold_in(key, 21)
    key_place = jax.random.fold_in(key, 22)
    values = jax.random.randint(key_values, (CH * K,), 0, DLOC)
    place = jax.random.randint(key_place, (), 0, CH * K)
    values = values.at[place].set(DLOC - 1)
    return values.reshape(CH, K).astype(jnp.int32)


def draw_level_shifts(key, part):
    layers = []
    for level in range(XLEV):
        bound = DLOC * 2 ** level // 2
        key_values = jax.random.fold_in(key, 100 + level)
        key_place = jax.random.fold_in(key, 200 + level)
        values = jax.random.randint(key_values, (DMS,), 0, bound)
        place = jax.random.randint(key_place, (), 0, DMS)
        layers.append(values.at[place].set(bound - 1))
    return jnp.stack(layers).astype(jnp.int32)


def draw_box_widths(key, part):
    lowest = 2 ** jnp.arange(NW, dtype=jnp.int32)
    extra = jax.random.randint(jax.random.fold_in(key, 31), (NW,), 0, 2 ** 20) % lowest
    widths = lowest + extra
    widths = widths.at[NW - 1].set(WMAX)
    return widths.astype(jnp.int32)


def set_ends(result, rng, low, largest):
    extent = result.shape
    spot = [jax.random.randint(jax.random.fold_in(rng, axis), (), 0, extent[axis]) for axis in range(len(extent))]
    result = result.at[tuple(spot)].set(low)
    longest = extent.index(max(extent))
    spot[longest] = (spot[longest] + 1) % extent[longest]
    return result.at[tuple(spot)].set(largest)


def setup_inputs(seed: int = 0, part: int = 0) -> dict:
    seeds = jax.random.split(jax.random.key(seed), 7)
    part_splits = jax.random.split(jax.random.fold_in(seeds[6], part), 7)
    filterbank = draw_filterbank(jax.random.fold_in(jax.random.fold_in(seeds[6], part), 71), part)
    local_delays = draw_local_delays(jax.random.fold_in(seeds[6], 71), part)
    lower_rows = set_ends(jax.random.randint(seeds[2], (XLEV, DMS), 0, K), jax.random.fold_in(seeds[2], 1), 0, K - 1).astype(jnp.int32)
    upper_rows = set_ends(jax.random.randint(seeds[3], (XLEV, DMS), 0, K), jax.random.fold_in(seeds[3], 1), 0, K - 1).astype(jnp.int32)
    level_shifts = draw_level_shifts(jax.random.fold_in(seeds[6], 71), part)
    box_widths = draw_box_widths(jax.random.fold_in(seeds[6], 71), part)
    return dict(filterbank=filterbank, local_delays=local_delays, lower_rows=lower_rows, upper_rows=upper_rows, level_shifts=level_shifts, box_widths=box_widths)


def delay_rows(series, shift_by, reach_now):
    length = series.shape[1]
    padded = jnp.pad(series, ((0, 0), (reach_now, 0)))

    def take_one(single, amount):
        return lax.dynamic_slice_in_dim(single, reach_now - amount, length, 0)
    return jax.vmap(take_one)(padded, shift_by)

def reference(filterbank, local_delays, lower_rows, upper_rows, level_shifts, box_widths):
    samples = filterbank.shape[1]
    channel_rows = filterbank.astype(jnp.float32).reshape(N_CHAN, CH_DEV, samples).transpose(1, 0, 2)
    channel_delays = local_delays.reshape(N_CHAN, CH_DEV, K).transpose(1, 0, 2)

    def block_series(single, amounts):
        padded = jnp.pad(single, (DLOC, 0))

        def take_one(amount):
            return lax.dynamic_slice_in_dim(padded, DLOC - amount, samples, 0)
        return jax.vmap(take_one)(amounts)

    def add_channel(summed, chan_item):
        rows_now, delays_now = chan_item
        return (summed + jax.vmap(block_series)(rows_now, delays_now), None)
    state, _ = lax.scan(add_channel, jnp.zeros((N_CHAN, K, samples), jnp.float32), (channel_rows, channel_delays))
    blocks = jnp.arange(N_CHAN, dtype=jnp.int32)
    for level in range(XLEV):
        bit_value = 2 ** level
        reach_now = DLOC * bit_value // 2
        low_block = blocks - (blocks & bit_value)
        high_block = low_block + bit_value
        low_index = lower_rows[level].reshape(N_CHAN, K)
        high_index = upper_rows[level].reshape(N_CHAN, K)
        shifts_now = level_shifts[level].reshape(N_CHAN * K)
        picked_low = state[low_block[:, None], low_index]
        picked_high = state[high_block[:, None], high_index].reshape(N_CHAN * K, samples)
        state = picked_low + delay_rows(picked_high, shifts_now, reach_now).reshape(N_CHAN, K, samples)
    series = state.reshape(N_CHAN * K, samples)
    mean_square = lax.optimization_barrier(jnp.mean(series * series, axis=1))
    inverse_rms = lax.rsqrt(mean_square + 1e-05)
    running = jnp.cumsum(jnp.pad(series, ((0, 0), (WMAX, 0))), axis=1)
    later_sum = running[:, WMAX:]

    def one_width(box_width):
        earlier = lax.dynamic_slice_in_dim(running, WMAX - box_width, samples, 1)
        return (later_sum - earlier) * inverse_rms[:, None] / jnp.sqrt(box_width.astype(jnp.float32))
    return lax.map(one_width, box_widths)
```

```python
import functools

import jax
import jax.numpy as jnp
from jax import lax
from jax.experimental import pallas as pl
from jax.experimental.pallas import tpu as pltpu
from jax.sharding import PartitionSpec as P

DLOC = 64
LANES = 128
FINE = 8
COARSE = DLOC // FINE
CHUNKS = 3
PACKED = 16
TILES = (1024, 896, 768, 640, 512, 384, 256, 128)
SHARED = 6
FIRST = 4
STEPS = [
    ("sum", 0),
    ("meet",),
    ("send", 0),
    ("share",),
    ("sum", 2, True),
    ("send", 2),
    ("rim",),
    ("merge", 0, 0),
    ("sum", 1),
    ("send", 1),
    ("merge", 0, 2),
    ("merge", 0, 3),
    ("relay",),
    ("merge", 0, 1),
    ("merge", 1, 0),
    ("merge", 1, 2),
    ("merge", 1, 1),
    ("merge", 1, 3),
    ("far", 0),
    ("merge", 2, 0),
    ("far", 1),
    ("merge", 2, 2),
    ("merge", 2, 3),
    ("merge", 2, 1),
]
MESH = pl.DeviceIdType.MESH


def lane_up(count):
    return -(-count // LANES) * LANES


def code_rows(rows):
    largest = jnp.maximum(jnp.max(jnp.abs(rows), axis=1, keepdims=True), 2.0**-100)
    exponent = jnp.floor(jnp.log2(largest))
    coded = jnp.round(jnp.clip(rows * jnp.exp2(14.0 - exponent), -32767.0, 32767.0))
    at = lax.broadcasted_iota(jnp.int32, (rows.shape[0], LANES), 0)
    to = lax.broadcasted_iota(jnp.int32, (rows.shape[0], LANES), 1)
    along = jnp.sum(jnp.where(at == to, exponent, 0.0), axis=0, keepdims=True)
    along = jnp.broadcast_to(along, (PACKED, LANES))
    return coded.astype(jnp.int32).astype(jnp.int16), along.astype(jnp.int32).astype(jnp.int16)


def decode_rows(coded, along):
    values = coded.astype(jnp.int32).astype(jnp.float32)
    exponents = along.astype(jnp.int32)[:1, : coded.shape[0]]
    return values * jnp.exp2(as_column(exponents).astype(jnp.float32) - 14.0)


def as_column(row):
    count = row.shape[1]
    at = lax.broadcasted_iota(jnp.int32, (count, count), 0)
    to = lax.broadcasted_iota(jnp.int32, (count, count), 1)
    spread = jnp.where(at == to, row.astype(jnp.float32), 0.0)
    return jnp.sum(spread, axis=1, keepdims=True).astype(jnp.int32)


def split(source):
    high = source.astype(jnp.bfloat16)
    low = (source - high.astype(jnp.float32)).astype(jnp.bfloat16)
    return high, low


def choose(lower, upper, upper_side):
    rows = lower.shape[0]
    at = lax.broadcasted_iota(jnp.int32, (rows, 2 * rows), 1)
    at = jnp.where(at >= rows, at - rows, at)
    low = jnp.where(at == lower, 1.0, 0.0)
    high = jnp.where(at == upper, 1.0, 0.0)
    none = jnp.zeros_like(low)
    own_low = jnp.where(upper_side, none, low)
    own_high = jnp.where(upper_side, high, none)
    chosen = jnp.concatenate(
        [
            jnp.concatenate([own_low, low - own_low], axis=1),
            jnp.concatenate([own_high, high - own_high], axis=1),
        ],
        axis=0,
    )
    return chosen.astype(jnp.bfloat16)


def pick(chosen, own, partner):
    stacked = jnp.concatenate([*split(own), *split(partner)], axis=0)
    return jnp.dot(chosen, stacked, preferred_element_type=jnp.float32)


def delayed(moved, shifts, reach, room):
    for bit in range((reach - 1).bit_length()):
        moved = jnp.where((shifts >> bit) & 1 == 1, pltpu.roll(moved, 2**bit, 1), moved)
    return moved[:, room:]


def reach_of(level):
    return DLOC * 2**level // 2


class Plan:
    def __init__(self, widths, samples):
        tiles = [each // LANES for each in widths]
        self.levels = levels = len(widths) - 1
        self.width = widths[0]
        self.old = widths[0] - samples
        self.starts = starts = [tiles[0] - each for each in tiles]
        halo = tiles[0] - samples // LANES
        past = [sum(reach_of(each) - 1 for each in range(level)) for level in range(levels + 1)]
        if levels == 3 and samples // LANES >= 16:
            self.shared = SHARED
            back = -(-past[levels - 1] // LANES)
            middle = tiles[0] - SHARED
            first = halo + 1
            valid = [first + -(-each // LANES) for each in past]
            after = first + FIRST
            begins = [
                (valid[levels] * LANES - past[levels] + past[level]) // LANES
                for level in range(levels + 1)
            ]
            spans = [
                [
                    (begins[level], after),
                    (starts[level], valid[level]),
                    (after, middle),
                    (middle, tiles[0]),
                ]
                for level in range(levels + 1)
            ]
            self.far = (middle - back, tiles[0])
            self.steps = STEPS
        else:
            self.shared = 0
            fair = (tiles[0] - 1) // CHUNKS
            most = (tiles[-1] - 1) // max(CHUNKS - 1, 1)
            later = min(fair, most) // 2 * 2 or 1
            sizes = [tiles[0] - later * (CHUNKS - 1)] + [later] * (CHUNKS - 1)
            edges = [sum(sizes[:count]) for count in range(CHUNKS + 1)]
            spans = [
                [(max(edges[c], start), edges[c + 1]) for c in range(CHUNKS)] for start in starts
            ]
            self.far = (0, 0)
            self.steps = [("meet",), ("rim",)]
            for turn in range(CHUNKS + levels):
                if turn < CHUNKS:
                    self.steps += [("sum", turn), ("send", turn)]
                self.steps += [
                    ("merge", level, turn - 1 - level)
                    for level in range(levels)
                    if 0 <= turn - 1 - level < CHUNKS
                ]
        self.spans = [[(LANES * b, LANES * e) for b, e in row] for row in spans]
        self.far = tuple(LANES * each for each in self.far)
        self.chunks = len(self.spans[0])

    def size(self, level, chunk):
        begin, end = self.spans[level][chunk]
        return end - begin

    def sends(self, level, chunk):
        return not (self.shared and level == self.levels - 1 and chunk == self.chunks - 1)


def sweep_kernel(
    plan,
    rim,
    fb_ref,
    delays_hbm,
    lower_hbm,
    upper_hbm,
    shifts_hbm,
    widths_hbm,
    state_ref,
    squares_ref,
    widths_ref,
    delays_ref,
    lower_ref,
    upper_ref,
    shifts_ref,
    widths_row,
    ext,
    rim_in,
    onehot,
    spread,
    partial,
    owns,
    parts,
    picked,
    outgoing,
    incoming,
    scale_out,
    scale_in,
    square_out,
    square_in,
    local_sem,
    small_sem,
    pair_send,
    pair_recv,
    send_sem,
    recv_sem,
    scale_send,
    scale_recv,
    *far,
):
    channels, samples = fb_ref.shape
    rows = delays_ref.shape[0]
    levels, chunks, spans, width = plan.levels, plan.chunks, plan.spans, plan.width
    top = levels - 1
    total = rim + samples
    skip = total - width
    tail = picked[0].shape[1] - width
    sent_rim = min(rim, samples)
    empty = LANES + rim - sent_rim

    chan = lax.axis_index("chan")
    tm = lax.axis_index("tm")
    sides = [lax.rem(lax.div(chan, 1 << level), 2) for level in range(levels)]
    partners = [
        {"chan": chan + (1 << level) - (2 << level) * sides[level]} for level in range(levels)
    ]
    pair = {"tm": 1 - tm}

    barrier = pltpu.get_barrier_semaphore()
    for device in [pair] + partners:
        pl.semaphore_signal(barrier, inc=1, device_id=device, device_id_type=MESH)
    own_copy = pltpu.make_async_copy(fb_ref, ext.at[:, pl.ds(LANES + rim, samples)], local_sem)
    small_copies = [
        pltpu.make_async_copy(source, target, small_sem.at[at])
        for at, (source, target) in enumerate(
            [
                (delays_hbm, delays_ref),
                (lower_hbm, lower_ref),
                (upper_hbm, upper_ref),
                (shifts_hbm, shifts_ref),
                (widths_hbm, widths_row),
            ]
        )
    ]
    for copy in small_copies:
        copy.start()
    own_copy.start()

    def remote(source, target, sent, received, device):
        return pltpu.make_async_remote_copy(
            src_ref=source,
            dst_ref=target,
            send_sem=sent,
            recv_sem=received,
            device_id=device,
            device_id_type=MESH,
        )

    rim_copy = remote(
        fb_ref.at[:, pl.ds(samples - sent_rim, sent_rim)],
        rim_in,
        pair_send.at[0],
        pair_recv.at[0],
        pair,
    )

    ext[:, : LANES + rim] = jnp.zeros((channels, LANES + rim), jnp.bfloat16)
    for level in range(levels):
        picked[level][:, :tail] = jnp.zeros((rows, tail), jnp.float32)
        begin = tail + spans[level][0][0]
        if begin > tail:
            picked[level][:, begin - tail : begin] = jnp.zeros((rows, tail), jnp.float32)
    for copy in small_copies:
        copy.wait()
    widths_ref[...] = jnp.broadcast_to(as_column(widths_row[...]), widths_ref.shape)
    for coarse in range(COARSE):
        relative = delays_ref[...] - FINE * coarse
        for fine in range(FINE):
            onehot[coarse * rows : (coarse + 1) * rows, fine * channels : (fine + 1) * channels] = (
                jnp.where(relative == fine, 1.0, 0.0).astype(jnp.bfloat16)
            )

    def column_of(ref, level):
        return as_column(ref[level : level + 1, :])

    chosen = [
        choose(column_of(lower_ref, level), column_of(upper_ref, level), sides[level] == 1)
        for level in range(levels)
    ]
    shifts = [column_of(shifts_ref, level) for level in range(levels)]

    def history(level, chunk):
        begin, end = spans[level][chunk]
        return min(max(plan.old - begin, 0), end - begin)

    def exchange(level, chunk, act):
        if not plan.sends(level, chunk):
            return
        old = history(level, chunk)
        size = plan.size(level, chunk)

        def columns(begin):
            act(
                remote(
                    outgoing[level][chunk].at[:, pl.ds(begin, size - begin)],
                    incoming[level][chunk].at[:, pl.ds(begin, size - begin)],
                    send_sem.at[level, chunk],
                    recv_sem.at[level, chunk],
                    partners[level],
                )
            )

        act(
            remote(
                scale_out.at[level, chunk],
                scale_in.at[level, chunk],
                scale_send.at[level, chunk],
                scale_recv.at[level, chunk],
                partners[level],
            )
        )
        if old:
            pl.when(tm > 0)(lambda: columns(0))
            if old < size:
                pl.when(tm == 0)(lambda: columns(old))
        else:
            columns(0)

    def start(copy):
        copy.start()

    def hand_on(level, chunk, values):
        begin, end = spans[level][chunk]
        owns[level][:, begin:end] = values
        if plan.sends(level, chunk):
            outgoing[level][chunk][...], scale_out[level, chunk] = code_rows(values)

    @pl.when(tm == 0)
    def _():
        for level in range(levels):
            for chunk in range(chunks):
                old = history(level, chunk)
                if old and plan.sends(level, chunk):
                    incoming[level][chunk][:, :old] = jnp.zeros((rows, old), jnp.int16)

    def dedisperse(begin, end, known):
        first = skip + begin - (0 if known else LANES)
        tile = next(t for t in TILES if (skip + end - first) % t == 0)

        def step(index, carry):
            start = pl.multiple_of(first + index * tile, LANES)
            window = ext[:, pl.ds(start, tile + LANES)]
            for fine in range(FINE):
                spread[fine * channels : (fine + 1) * channels, :tile] = window[
                    :, LANES - fine : LANES - fine + tile
                ]
            partial[:, pl.ds(start, tile)] = jnp.dot(
                onehot[...], spread[:, :tile], preferred_element_type=jnp.float32
            )
            return carry

        lax.fori_loop(0, (skip + end - first) // tile, step, 0)
        summed = None
        for coarse in range(COARSE):
            back = skip - FINE * coarse
            term = partial[coarse * rows : (coarse + 1) * rows, back + begin : back + end]
            summed = term if summed is None else summed + term
        return summed

    def merge(level, chunk):
        begin, end = spans[level][chunk]
        after, close = spans[level + 1][chunk]
        if plan.sends(level, chunk):
            exchange(level, chunk, lambda copy: copy.wait_recv())
            parts[level][:, begin:end] = decode_rows(
                incoming[level][chunk][...], scale_in[level, chunk]
            )
        begin = min(begin, after)
        both = pick(chosen[level], owns[level][:, begin:close], parts[level][:, begin:close])
        picked[level][:, tail + begin : tail + close] = both[rows:]
        room = lane_up(reach_of(level))
        moved = picked[level][:, tail + after - room : tail + close]
        return both[:rows, after - begin :] + delayed(moved, shifts[level], reach_of(level), room)

    if plan.shared:
        (
            tables_out,
            tables_in,
            far_owns,
            far_parts,
            far_picked,
            far_coded,
            far_incoming,
            far_scale_out,
            far_scale_in,
            far_send,
            far_recv,
            far_scale_send,
            far_scale_recv,
        ) = far
        far_begin, far_end = plan.far
        middle = spans[0][chunks - 1][0]
        for level in range(top):
            far_picked[level][:, :tail] = jnp.zeros((rows, tail), jnp.float32)
            tables_out[3 * level : 3 * level + 1, :] = lower_ref[level : level + 1, :]
            tables_out[3 * level + 1 : 3 * level + 2, :] = upper_ref[level : level + 1, :]
            tables_out[3 * level + 2 : 3 * level + 3, :] = shifts_ref[level : level + 1, :]

    def far_copies(step):
        device = partners[top] if step == 0 else partners[step - 1]
        source = far_incoming[0] if step == 1 else far_coded[step]
        scales = far_scale_in.at[0] if step == 1 else far_scale_out.at[step]
        copies = [
            remote(scales, far_scale_in.at[step], far_scale_send.at[step], far_scale_recv.at[step], device),
            remote(source, far_incoming[step], far_send.at[step], far_recv.at[step], device),
        ]
        if step == 0:
            copies.append(remote(tables_out, tables_in, far_send.at[top + 1], far_recv.at[top + 1], device))
        return copies

    def far_start(step):
        for copy in far_copies(step):
            copy.start()

    def far_wait(step):
        for copy in far_copies(step):
            copy.wait_recv()
        return decode_rows(far_incoming[step][...], far_scale_in[step])

    def far_merge(level):
        far_parts[level][...] = far_wait(level + 1)
        lower, upper, later = (
            as_column(tables_in[3 * level + at : 3 * level + at + 1, :]) for at in range(3)
        )
        both = pick(
            choose(lower, upper, sides[level] == 1), far_owns[level][...], far_parts[level][...]
        )
        far_picked[level][:, tail:] = both[rows:]
        room = lane_up(reach_of(level))
        moved = far_picked[level][:, tail - room :]
        return both[:rows] + delayed(moved, later, reach_of(level), room)

    own_copy.wait()
    squares = jnp.zeros((rows, 1), jnp.float32)
    for step in plan.steps:
        kind = step[0]
        if kind == "meet":
            pl.semaphore_wait(barrier, levels + 1)
            rim_copy.start()
        elif kind == "rim":
            rim_copy.wait()
            ext[:, empty : LANES + rim] = jnp.where(
                tm == 0, jnp.zeros((channels, sent_rim), jnp.bfloat16), rim_in[...]
            )
        elif kind == "sum":
            begin, end = spans[0][step[1]]
            known = len(step) > 2 or begin + skip < LANES
            hand_on(0, step[1], dedisperse(begin, end, known))
        elif kind == "send":
            exchange(0, step[1], start)
        elif kind == "share":
            values = dedisperse(far_begin, far_end, len(step) > 1)
            owns[0][:, middle:far_end] = values[:, middle - far_begin :]
            coded, scales = code_rows(values)
            far_coded[0][...], far_scale_out[0] = coded, scales
            outgoing[0][chunks - 1][...] = coded[:, middle - far_begin :]
            scale_out[0, chunks - 1] = scales
            far_start(0)
            exchange(0, chunks - 1, start)
        elif kind == "relay":
            far_owns[0][...] = far_wait(0)
            far_start(1)
        elif kind == "far":
            level = step[1]
            values = far_merge(level)
            if level < top - 1:
                far_owns[level + 1][...] = values
                far_coded[level + 2][...], far_scale_out[level + 2] = code_rows(values)
                far_start(level + 2)
            else:
                parts[top][:, middle:far_end] = values[:, middle - far_begin :]
        else:
            _, level, chunk = step
            merged = merge(level, chunk)
            begin, end = spans[level + 1][chunk]
            if level < top:
                hand_on(level + 1, chunk, merged)
                exchange(level + 1, chunk, start)
            else:
                shown = spans[levels][chunk][0] - LANES * plan.starts[levels]
                state_ref[:, shown : shown + end - begin] = merged
                if end > plan.old:
                    fresh = merged[:, max(plan.old - begin, 0) :]
                    squares = squares + jnp.sum(fresh * fresh, axis=1, keepdims=True)
    square_out[...] = jnp.broadcast_to(squares, (rows, LANES))
    square_copy = remote(square_out, square_in, pair_send.at[1], pair_recv.at[1], pair)
    square_copy.start()
    for level in range(levels):
        for chunk in range(chunks):
            exchange(level, chunk, lambda copy: copy.wait_send())
    if plan.shared:
        for step in range(top + 1):
            for copy in far_copies(step):
                copy.wait_send()
    square_copy.wait()
    squares_ref[...] = square_out[...] + square_in[...]


def sweep(filterbank, delays, lower_rows, upper_rows, level_shifts, box_widths, widths):
    channels, samples = filterbank.shape
    rows = delays.shape[0]
    plan = Plan(widths, samples)
    levels, chunks, width = plan.levels, plan.chunks, plan.width
    rim = lane_up(width - samples + DLOC - 1)
    total = rim + samples

    def coded():
        return [
            [pltpu.VMEM((rows, plan.size(j, c)), jnp.int16) for c in range(chunks)]
            for j in range(levels)
        ]

    tail = lane_up(reach_of(levels - 1))
    scales = pltpu.VMEM((levels, chunks, PACKED, LANES), jnp.int16)
    vmem = pl.BlockSpec(memory_space=pltpu.VMEM)
    far = []
    if plan.shared:
        size = plan.far[1] - plan.far[0]
        far = [
            pltpu.VMEM((3 * (levels - 1), rows), jnp.int32),
            pltpu.VMEM((3 * (levels - 1), rows), jnp.int32),
            [pltpu.VMEM((rows, size), jnp.float32) for _ in range(levels - 1)],
            [pltpu.VMEM((rows, size), jnp.float32) for _ in range(levels - 1)],
            [pltpu.VMEM((rows, tail + size), jnp.float32) for _ in range(levels - 1)],
            [pltpu.VMEM((rows, size), jnp.int16) for _ in range(levels)],
            [pltpu.VMEM((rows, size), jnp.int16) for _ in range(levels)],
            pltpu.VMEM((levels, PACKED, LANES), jnp.int16),
            pltpu.VMEM((levels, PACKED, LANES), jnp.int16),
            pltpu.SemaphoreType.DMA((levels + 1,)),
            pltpu.SemaphoreType.DMA((levels + 1,)),
            pltpu.SemaphoreType.DMA((levels,)),
            pltpu.SemaphoreType.DMA((levels,)),
        ]
    return pl.pallas_call(
        functools.partial(sweep_kernel, plan, rim),
        name="sweep",
        out_shape=(
            jax.ShapeDtypeStruct((rows, widths[-1]), jnp.float32),
            jax.ShapeDtypeStruct((rows, LANES), jnp.float32),
            jax.ShapeDtypeStruct((box_widths.shape[0], LANES), jnp.int32),
        ),
        in_specs=[pl.BlockSpec(memory_space=pltpu.HBM)] * 6,
        out_specs=(vmem, vmem, vmem),
        scratch_shapes=[
            pltpu.VMEM(delays.shape, jnp.int32),
            pltpu.VMEM(lower_rows.shape, jnp.int32),
            pltpu.VMEM(upper_rows.shape, jnp.int32),
            pltpu.VMEM(level_shifts.shape, jnp.int32),
            pltpu.VMEM((1, box_widths.shape[0]), jnp.int32),
            pltpu.VMEM((channels, LANES + total), jnp.bfloat16),
            pltpu.VMEM((channels, min(rim, samples)), jnp.bfloat16),
            pltpu.VMEM((COARSE * rows, FINE * channels), jnp.bfloat16),
            pltpu.VMEM((FINE * channels, TILES[0]), jnp.bfloat16),
            pltpu.VMEM((COARSE * rows, total), jnp.float32),
            [pltpu.VMEM((rows, width), jnp.float32) for _ in range(levels)],
            [pltpu.VMEM((rows, width), jnp.float32) for _ in range(levels)],
            [pltpu.VMEM((rows, tail + width), jnp.float32) for _ in range(levels)],
            coded(),
            coded(),
            scales,
            scales,
            pltpu.VMEM((rows, LANES), jnp.float32),
            pltpu.VMEM((rows, LANES), jnp.float32),
            pltpu.SemaphoreType.DMA,
            pltpu.SemaphoreType.DMA((5,)),
            pltpu.SemaphoreType.DMA((2,)),
            pltpu.SemaphoreType.DMA((2,)),
            pltpu.SemaphoreType.DMA((levels, chunks)),
            pltpu.SemaphoreType.DMA((levels, chunks)),
            pltpu.SemaphoreType.DMA((levels, chunks)),
            pltpu.SemaphoreType.DMA((levels, chunks)),
            *far,
        ],
        compiler_params=pltpu.CompilerParams(
            collective_id=0, has_side_effects=True, vmem_limit_bytes=48 * 2**20
        ),
    )(
        *[
            pltpu.with_memory_space_constraint(each, pltpu.HBM)
            for each in (filterbank, delays, lower_rows, upper_rows, level_shifts, box_widths[None])
        ]
    )


def box_kernel(times, widths_ref, state_ref, squares_ref, out_ref, stacked):
    rows = state_ref.shape[0]
    tiles = out_ref.shape[2] // LANES
    per_step = out_ref.shape[0]

    @pl.when(pl.program_id(0) == 0)
    def _():
        for tile in range(tiles):
            part = state_ref[:, tile * LANES : (tile + 2) * LANES]
            high = part.astype(jnp.bfloat16)
            low = (part - high.astype(jnp.float32)).astype(jnp.bfloat16)
            stacked[tile * rows : (tile + 1) * rows, : 2 * LANES] = high
            stacked[tile * rows : (tile + 1) * rows, 2 * LANES :] = low

    inverse = lax.rsqrt(squares_ref[...] / times + 1e-05)
    masks = []
    factors = []
    for which in range(per_step):
        box_width = widths_ref[pl.ds(pl.program_id(0) * per_step + which, 1), :]
        at = lax.broadcasted_iota(jnp.int32, (2 * LANES, LANES), 0) - LANES
        to = lax.broadcasted_iota(jnp.int32, (2 * LANES, LANES), 1)
        inside = (at <= to) & (at > to - box_width)
        mask = jnp.where(inside, 1.0, 0.0).astype(jnp.bfloat16)
        masks.append(jnp.concatenate([mask, mask], axis=0))
        root = jnp.sqrt(box_width.astype(jnp.float32))
        factors.append(inverse / root)
    boxes = jnp.dot(
        stacked[...], jnp.concatenate(masks, axis=1), preferred_element_type=jnp.float32
    )
    for which in range(per_step):
        for tile in range(tiles):
            out_ref[which, :, tile * LANES : (tile + 1) * LANES] = (
                boxes[tile * rows : (tile + 1) * rows, which * LANES : (which + 1) * LANES]
                * factors[which]
            )


def box_filter(widths, state, squares, samples, times):
    rows = state.shape[0]
    count = widths.shape[0]
    per_step = 2 if count % 2 == 0 else 1
    return pl.pallas_call(
        functools.partial(box_kernel, times),
        name="boxes",
        grid=(count // per_step,),
        out_shape=jax.ShapeDtypeStruct((count, rows, samples), jnp.float32),
        in_specs=[
            pl.BlockSpec(memory_space=pltpu.VMEM),
            pl.BlockSpec(memory_space=pltpu.VMEM),
            pl.BlockSpec(memory_space=pltpu.VMEM),
        ],
        out_specs=pl.BlockSpec((per_step, rows, samples), lambda i: (i, 0, 0)),
        scratch_shapes=[pltpu.VMEM((samples // LANES * rows, 4 * LANES), jnp.bfloat16)],
        compiler_params=pltpu.CompilerParams(vmem_limit_bytes=32 * 2**20),
    )(widths, state, squares)


def local(filterbank, local_delays, lower_rows, upper_rows, level_shifts, box_widths):
    samples = filterbank.shape[1]
    levels = lax.axis_size("chan").bit_length() - 1
    needs = [LANES]
    for level in reversed(range(levels)):
        needs.insert(0, needs[0] - (level == levels - 1) + DLOC * 2**level // 2 - 1)
    widths = [samples + lane_up(need + 1) for need in needs[:-1]] + [samples + LANES]
    state, squares, spans = sweep(
        filterbank, local_delays.T, lower_rows, upper_rows, level_shifts, box_widths, widths
    )
    return box_filter(spans, state, squares, samples, samples * lax.axis_size("tm"))


def solution(mesh):
    placed = (
        P(("beam", "chan"), "tm"),
        P("chan", None),
        P(None, "chan"),
        P(None, "chan"),
        P(None, "chan"),
        P(),
    )
    return jax.shard_map(
        local,
        mesh=mesh,
        in_specs=placed,
        out_specs=P(None, ("beam", "chan"), "tm"),
        check_vma=False,
    )
```

```python
import functools

import jax
import jax.numpy as jnp
from jax import lax
from jax.experimental import pallas as pl
from jax.experimental.pallas import tpu as pltpu
from jax.sharding import PartitionSpec as P

DLOC = 64
LANES = 128
FINE = 8
COARSE = DLOC // FINE
CHUNKS = 3
PACKED = 16
TILES = (1024, 896, 768, 640, 512, 384, 256, 128)
SHARED = 6
FIRST = 4
STEPS = [
    ("sum", 0),
    ("meet",),
    ("send", 0),
    ("share",),
    ("sum", 2, True),
    ("send", 2),
    ("rim",),
    ("merge", 0, 0),
    ("sum", 1),
    ("send", 1),
    ("merge", 0, 2),
    ("merge", 0, 3),
    ("relay",),
    ("merge", 0, 1),
    ("merge", 1, 0),
    ("merge", 1, 2),
    ("merge", 1, 1),
    ("merge", 1, 3),
    ("far", 0),
    ("merge", 2, 0),
    ("far", 1),
    ("merge", 2, 2),
    ("merge", 2, 3),
    ("merge", 2, 1),
]
MESH = pl.DeviceIdType.MESH


def lane_up(count):
    return -(-count // LANES) * LANES


def code_rows(rows):
    largest = jnp.maximum(jnp.max(jnp.abs(rows), axis=1, keepdims=True), 2.0**-100)
    exponent = jnp.floor(jnp.log2(largest))
    coded = jnp.round(jnp.clip(rows * jnp.exp2(14.0 - exponent), -32767.0, 32767.0))
    at = lax.broadcasted_iota(jnp.int32, (rows.shape[0], LANES), 0)
    to = lax.broadcasted_iota(jnp.int32, (rows.shape[0], LANES), 1)
    along = jnp.sum(jnp.where(at == to, exponent, 0.0), axis=0, keepdims=True)
    along = jnp.broadcast_to(along, (PACKED, LANES))
    return coded.astype(jnp.int32).astype(jnp.int16), along.astype(jnp.int32).astype(jnp.int16)


def decode_rows(coded, along):
    values = coded.astype(jnp.int32).astype(jnp.float32)
    exponents = along.astype(jnp.int32)[:1, : coded.shape[0]]
    return values * jnp.exp2(as_column(exponents).astype(jnp.float32) - 14.0)


def as_column(row):
    count = row.shape[1]
    at = lax.broadcasted_iota(jnp.int32, (count, count), 0)
    to = lax.broadcasted_iota(jnp.int32, (count, count), 1)
    spread = jnp.where(at == to, row.astype(jnp.float32), 0.0)
    return jnp.sum(spread, axis=1, keepdims=True).astype(jnp.int32)


def split(source):
    high = source.astype(jnp.bfloat16)
    low = (source - high.astype(jnp.float32)).astype(jnp.bfloat16)
    return high, low


def choose(lower, upper, upper_side):
    rows = lower.shape[0]
    at = lax.broadcasted_iota(jnp.int32, (rows, 2 * rows), 1)
    at = jnp.where(at >= rows, at - rows, at)
    low = jnp.where(at == lower, 1.0, 0.0)
    high = jnp.where(at == upper, 1.0, 0.0)
    none = jnp.zeros_like(low)
    own_low = jnp.where(upper_side, none, low)
    own_high = jnp.where(upper_side, high, none)
    chosen = jnp.concatenate(
        [
            jnp.concatenate([own_low, low - own_low], axis=1),
            jnp.concatenate([own_high, high - own_high], axis=1),
        ],
        axis=0,
    )
    return chosen.astype(jnp.bfloat16)


def pick(chosen, own, partner):
    stacked = jnp.concatenate([*split(own), *split(partner)], axis=0)
    return jnp.dot(chosen, stacked, preferred_element_type=jnp.float32)


def delayed(moved, shifts, reach, room):
    for bit in range(LANES.bit_length() - 1, (reach - 1).bit_length()):
        moved = jnp.where((shifts >> bit) & 1 == 1, pltpu.roll(moved, 2**bit, 1), moved)
    fine = shifts & (LANES - 1)
    lane = lax.broadcasted_iota(jnp.int32, (moved.shape[0], LANES), 1)
    index = (lane - fine) & (LANES - 1)
    early = lane < fine
    turned = [
        jnp.take_along_axis(
            moved[:, begin : begin + LANES], index, axis=1, mode="promise_in_bounds"
        )
        for begin in range(room - LANES, moved.shape[1], LANES)
    ]
    return jnp.concatenate(
        [jnp.where(early, before, now) for before, now in zip(turned, turned[1:])], axis=1
    )


def reach_of(level):
    return DLOC * 2**level // 2


class Plan:
    def __init__(self, widths, samples):
        tiles = [each // LANES for each in widths]
        self.levels = levels = len(widths) - 1
        self.width = widths[0]
        self.old = widths[0] - samples
        self.starts = starts = [tiles[0] - each for each in tiles]
        halo = tiles[0] - samples // LANES
        past = [sum(reach_of(each) - 1 for each in range(level)) for level in range(levels + 1)]
        if levels == 3 and samples // LANES >= 16:
            self.shared = SHARED
            back = -(-past[levels - 1] // LANES)
            middle = tiles[0] - SHARED
            first = halo + 1
            valid = [first + -(-each // LANES) for each in past]
            after = first + FIRST
            begins = [
                (valid[levels] * LANES - past[levels] + past[level]) // LANES
                for level in range(levels + 1)
            ]
            spans = [
                [
                    (begins[level], after),
                    (starts[level], valid[level]),
                    (after, middle),
                    (middle, tiles[0]),
                ]
                for level in range(levels + 1)
            ]
            self.far = (middle - back, tiles[0])
            self.steps = STEPS
        else:
            self.shared = 0
            fair = (tiles[0] - 1) // CHUNKS
            most = (tiles[-1] - 1) // max(CHUNKS - 1, 1)
            later = min(fair, most) // 2 * 2 or 1
            sizes = [tiles[0] - later * (CHUNKS - 1)] + [later] * (CHUNKS - 1)
            edges = [sum(sizes[:count]) for count in range(CHUNKS + 1)]
            spans = [
                [(max(edges[c], start), edges[c + 1]) for c in range(CHUNKS)] for start in starts
            ]
            self.far = (0, 0)
            self.steps = [("meet",), ("rim",)]
            for turn in range(CHUNKS + levels):
                if turn < CHUNKS:
                    self.steps += [("sum", turn), ("send", turn)]
                self.steps += [
                    ("merge", level, turn - 1 - level)
                    for level in range(levels)
                    if 0 <= turn - 1 - level < CHUNKS
                ]
        self.spans = [[(LANES * b, LANES * e) for b, e in row] for row in spans]
        self.far = tuple(LANES * each for each in self.far)
        self.chunks = len(self.spans[0])

    def size(self, level, chunk):
        begin, end = self.spans[level][chunk]
        return end - begin

    def sends(self, level, chunk):
        return not (self.shared and level == self.levels - 1 and chunk == self.chunks - 1)


def sweep_kernel(
    plan,
    rim,
    fb_ref,
    delays_hbm,
    lower_hbm,
    upper_hbm,
    shifts_hbm,
    widths_hbm,
    boxes_ref,
    squares_ref,
    widths_ref,
    state,
    masks,
    delays_ref,
    lower_ref,
    upper_ref,
    shifts_ref,
    widths_row,
    ext,
    rim_in,
    onehot,
    spread,
    partial,
    owns,
    parts,
    picked,
    outgoing,
    incoming,
    scale_out,
    scale_in,
    square_out,
    square_in,
    local_sem,
    small_sem,
    pair_send,
    pair_recv,
    send_sem,
    recv_sem,
    scale_send,
    scale_recv,
    *far,
):
    channels, samples = fb_ref.shape
    rows = delays_ref.shape[0]
    levels, chunks, spans, width = plan.levels, plan.chunks, plan.spans, plan.width
    top = levels - 1
    total = rim + samples
    skip = total - width
    tail = picked[0].shape[1] - width
    sent_rim = min(rim, samples)
    empty = LANES + rim - sent_rim

    chan = lax.axis_index("chan")
    tm = lax.axis_index("tm")
    sides = [lax.rem(lax.div(chan, 1 << level), 2) for level in range(levels)]
    partners = [
        {"chan": chan + (1 << level) - (2 << level) * sides[level]} for level in range(levels)
    ]
    pair = {"tm": 1 - tm}

    barrier = pltpu.get_barrier_semaphore()
    for device in [pair] + partners:
        pl.semaphore_signal(barrier, inc=1, device_id=device, device_id_type=MESH)
    own_copy = pltpu.make_async_copy(fb_ref, ext.at[:, pl.ds(LANES + rim, samples)], local_sem)
    small_copies = [
        pltpu.make_async_copy(source, target, small_sem.at[at])
        for at, (source, target) in enumerate(
            [
                (delays_hbm, delays_ref),
                (lower_hbm, lower_ref),
                (upper_hbm, upper_ref),
                (shifts_hbm, shifts_ref),
                (widths_hbm, widths_row),
            ]
        )
    ]
    for copy in small_copies:
        copy.start()
    own_copy.start()

    def remote(source, target, sent, received, device):
        return pltpu.make_async_remote_copy(
            src_ref=source,
            dst_ref=target,
            send_sem=sent,
            recv_sem=received,
            device_id=device,
            device_id_type=MESH,
        )

    rim_copy = remote(
        fb_ref.at[:, pl.ds(samples - sent_rim, sent_rim)],
        rim_in,
        pair_send.at[0],
        pair_recv.at[0],
        pair,
    )

    ext[:, : LANES + rim] = jnp.zeros((channels, LANES + rim), jnp.bfloat16)
    for level in range(levels):
        picked[level][:, :tail] = jnp.zeros((rows, tail), jnp.float32)
        begin = tail + spans[level][0][0]
        if begin > tail:
            picked[level][:, begin - tail : begin] = jnp.zeros((rows, tail), jnp.float32)
    for copy in small_copies:
        copy.wait()
    spans_now = jnp.broadcast_to(as_column(widths_row[...]), widths_ref.shape)
    widths_ref[...] = spans_now
    at = lax.broadcasted_iota(jnp.int32, (2 * LANES, LANES), 0) - LANES
    to = lax.broadcasted_iota(jnp.int32, (2 * LANES, LANES), 1)
    for which in range(widths_ref.shape[0]):
        inside = (at <= to) & (at > to - spans_now[which : which + 1, :])
        masks[:, which * LANES : (which + 1) * LANES] = jnp.where(inside, 1.0, 0.0).astype(
            jnp.bfloat16
        )
    for coarse in range(COARSE):
        relative = delays_ref[...] - FINE * coarse
        for fine in range(FINE):
            onehot[coarse * rows : (coarse + 1) * rows, fine * channels : (fine + 1) * channels] = (
                jnp.where(relative == fine, 1.0, 0.0).astype(jnp.bfloat16)
            )

    def column_of(ref, level):
        return as_column(ref[level : level + 1, :])

    chosen = [
        choose(column_of(lower_ref, level), column_of(upper_ref, level), sides[level] == 1)
        for level in range(levels)
    ]
    shifts = [column_of(shifts_ref, level) for level in range(levels)]

    def history(level, chunk):
        begin, end = spans[level][chunk]
        return min(max(plan.old - begin, 0), end - begin)

    def exchange(level, chunk, act):
        if not plan.sends(level, chunk):
            return
        old = history(level, chunk)
        size = plan.size(level, chunk)

        def columns(begin):
            act(
                remote(
                    outgoing[level][chunk].at[:, pl.ds(begin, size - begin)],
                    incoming[level][chunk].at[:, pl.ds(begin, size - begin)],
                    send_sem.at[level, chunk],
                    recv_sem.at[level, chunk],
                    partners[level],
                )
            )

        act(
            remote(
                scale_out.at[level, chunk],
                scale_in.at[level, chunk],
                scale_send.at[level, chunk],
                scale_recv.at[level, chunk],
                partners[level],
            )
        )
        if old:
            pl.when(tm > 0)(lambda: columns(0))
            if old < size:
                pl.when(tm == 0)(lambda: columns(old))
        else:
            columns(0)

    def start(copy):
        copy.start()

    def hand_on(level, chunk, values):
        begin, end = spans[level][chunk]
        owns[level][:, begin:end] = values
        if plan.sends(level, chunk):
            outgoing[level][chunk][...], scale_out[level, chunk] = code_rows(values)

    @pl.when(tm == 0)
    def _():
        for level in range(levels):
            for chunk in range(chunks):
                old = history(level, chunk)
                if old and plan.sends(level, chunk):
                    incoming[level][chunk][:, :old] = jnp.zeros((rows, old), jnp.int16)

    def dedisperse(begin, end, known):
        first = skip + begin - (0 if known else LANES)
        tile = next(t for t in TILES if (skip + end - first) % t == 0)

        def step(index, carry):
            start = pl.multiple_of(first + index * tile, LANES)
            window = ext[:, pl.ds(start, tile + LANES)]
            for fine in range(FINE):
                spread[fine * channels : (fine + 1) * channels, :tile] = window[
                    :, LANES - fine : LANES - fine + tile
                ]
            partial[:, pl.ds(start, tile)] = jnp.dot(
                onehot[...], spread[:, :tile], preferred_element_type=jnp.float32
            )
            return carry

        lax.fori_loop(0, (skip + end - first) // tile, step, 0)
        summed = None
        for coarse in range(COARSE):
            back = skip - FINE * coarse
            term = partial[coarse * rows : (coarse + 1) * rows, back + begin : back + end]
            summed = term if summed is None else summed + term
        return summed

    def merge(level, chunk):
        begin, end = spans[level][chunk]
        after, close = spans[level + 1][chunk]
        if plan.sends(level, chunk):
            exchange(level, chunk, lambda copy: copy.wait_recv())
            parts[level][:, begin:end] = decode_rows(
                incoming[level][chunk][...], scale_in[level, chunk]
            )
        begin = min(begin, after)
        both = pick(chosen[level], owns[level][:, begin:close], parts[level][:, begin:close])
        picked[level][:, tail + begin : tail + close] = both[rows:]
        room = lane_up(reach_of(level))
        moved = picked[level][:, tail + after - room : tail + close]
        return both[:rows, after - begin :] + delayed(moved, shifts[level], reach_of(level), room)

    if plan.shared:
        (
            tables_out,
            tables_in,
            far_owns,
            far_parts,
            far_picked,
            far_coded,
            far_incoming,
            far_scale_out,
            far_scale_in,
            far_send,
            far_recv,
            far_scale_send,
            far_scale_recv,
        ) = far
        far_begin, far_end = plan.far
        middle = spans[0][chunks - 1][0]
        for level in range(top):
            far_picked[level][:, :tail] = jnp.zeros((rows, tail), jnp.float32)
            tables_out[3 * level : 3 * level + 1, :] = lower_ref[level : level + 1, :]
            tables_out[3 * level + 1 : 3 * level + 2, :] = upper_ref[level : level + 1, :]
            tables_out[3 * level + 2 : 3 * level + 3, :] = shifts_ref[level : level + 1, :]

    def far_copies(step):
        device = partners[top] if step == 0 else partners[step - 1]
        source = far_incoming[0] if step == 1 else far_coded[step]
        scales = far_scale_in.at[0] if step == 1 else far_scale_out.at[step]
        copies = [
            remote(scales, far_scale_in.at[step], far_scale_send.at[step], far_scale_recv.at[step], device),
            remote(source, far_incoming[step], far_send.at[step], far_recv.at[step], device),
        ]
        if step == 0:
            copies.append(remote(tables_out, tables_in, far_send.at[top + 1], far_recv.at[top + 1], device))
        return copies

    def far_start(step):
        for copy in far_copies(step):
            copy.start()

    def far_wait(step):
        for copy in far_copies(step):
            copy.wait_recv()
        return decode_rows(far_incoming[step][...], far_scale_in[step])

    def far_merge(level):
        far_parts[level][...] = far_wait(level + 1)
        lower, upper, later = (
            as_column(tables_in[3 * level + at : 3 * level + at + 1, :]) for at in range(3)
        )
        both = pick(
            choose(lower, upper, sides[level] == 1), far_owns[level][...], far_parts[level][...]
        )
        far_picked[level][:, tail:] = both[rows:]
        room = lane_up(reach_of(level))
        moved = far_picked[level][:, tail - room :]
        return both[:rows] + delayed(moved, later, reach_of(level), room)

    halo = plan.old // LANES
    offset = plan.starts[levels]

    def boxes(tiles):
        high, low = split(
            jnp.concatenate(
                [
                    state[:, LANES * (tile - 1 - offset) : LANES * (tile + 1 - offset)]
                    for tile in tiles
                ],
                axis=0,
            )
        )
        count = len(tiles) * rows
        for which in range(0, widths_ref.shape[0], 2):
            both = jnp.dot(
                jnp.concatenate([high, low], axis=0),
                masks[:, which * LANES : (which + 2) * LANES],
                preferred_element_type=jnp.float32,
            )
            summed = both[:count] + both[count:]
            for at, tile in enumerate(tiles):
                for each in range(2):
                    boxes_ref[which + each, :, LANES * (tile - halo) : LANES * (tile + 1 - halo)] = (
                        summed[at * rows : (at + 1) * rows, each * LANES : (each + 1) * LANES]
                    )

    def send_squares():
        square_out[...] = jnp.broadcast_to(squares, (rows, LANES))
        square_copy.start()

    square_copy = remote(square_out, square_in, pair_send.at[1], pair_recv.at[1], pair)
    finished, shown = set(), set()
    end_of_all = state.shape[1]
    own_copy.wait()
    squares = jnp.zeros((rows, 1), jnp.float32)
    for step in plan.steps:
        kind = step[0]
        if kind == "meet":
            pl.semaphore_wait(barrier, levels + 1)
            rim_copy.start()
        elif kind == "rim":
            rim_copy.wait()
            ext[:, empty : LANES + rim] = jnp.where(
                tm == 0, jnp.zeros((channels, sent_rim), jnp.bfloat16), rim_in[...]
            )
        elif kind == "sum":
            begin, end = spans[0][step[1]]
            known = len(step) > 2 or begin + skip < LANES
            hand_on(0, step[1], dedisperse(begin, end, known))
        elif kind == "send":
            exchange(0, step[1], start)
        elif kind == "share":
            values = dedisperse(far_begin, far_end, len(step) > 1)
            owns[0][:, middle:far_end] = values[:, middle - far_begin :]
            coded, scales = code_rows(values)
            far_coded[0][...], far_scale_out[0] = coded, scales
            outgoing[0][chunks - 1][...] = coded[:, middle - far_begin :]
            scale_out[0, chunks - 1] = scales
            far_start(0)
            exchange(0, chunks - 1, start)
        elif kind == "relay":
            far_owns[0][...] = far_wait(0)
            far_start(1)
        elif kind == "far":
            level = step[1]
            values = far_merge(level)
            if level < top - 1:
                far_owns[level + 1][...] = values
                far_coded[level + 2][...], far_scale_out[level + 2] = code_rows(values)
                far_start(level + 2)
            else:
                parts[top][:, middle:far_end] = values[:, middle - far_begin :]
        else:
            _, level, chunk = step
            merged = merge(level, chunk)
            begin, end = spans[level + 1][chunk]
            if level < top:
                hand_on(level + 1, chunk, merged)
                exchange(level + 1, chunk, start)
            else:
                state[:, begin - LANES * offset : end - LANES * offset] = merged
                if end > plan.old:
                    fresh = merged[:, max(plan.old - begin, 0) :]
                    squares = squares + jnp.sum(fresh * fresh, axis=1, keepdims=True)
                finished |= set(range(begin // LANES, end // LANES))
                if len(finished) * LANES == end_of_all:
                    send_squares()
                ready = sorted(
                    tile
                    for tile in finished - shown
                    if tile >= halo and tile - 1 in finished
                )
                shown |= set(ready)
                for at in range(0, len(ready), 4):
                    boxes(ready[at : at + 4])
    for level in range(levels):
        for chunk in range(chunks):
            exchange(level, chunk, lambda copy: copy.wait_send())
    if plan.shared:
        for step in range(top + 1):
            for copy in far_copies(step):
                copy.wait_send()
    square_copy.wait()
    squares_ref[...] = square_out[...] + square_in[...]


def sweep(filterbank, delays, lower_rows, upper_rows, level_shifts, box_widths, widths):
    channels, samples = filterbank.shape
    rows = delays.shape[0]
    plan = Plan(widths, samples)
    levels, chunks, width = plan.levels, plan.chunks, plan.width
    rim = lane_up(width - samples + DLOC - 1)
    total = rim + samples

    def coded():
        return [
            [pltpu.VMEM((rows, plan.size(j, c)), jnp.int16) for c in range(chunks)]
            for j in range(levels)
        ]

    tail = lane_up(reach_of(levels - 1))
    scales = pltpu.VMEM((levels, chunks, PACKED, LANES), jnp.int16)
    vmem = pl.BlockSpec(memory_space=pltpu.VMEM)
    far = []
    if plan.shared:
        size = plan.far[1] - plan.far[0]
        far = [
            pltpu.VMEM((3 * (levels - 1), rows), jnp.int32),
            pltpu.VMEM((3 * (levels - 1), rows), jnp.int32),
            [pltpu.VMEM((rows, size), jnp.float32) for _ in range(levels - 1)],
            [pltpu.VMEM((rows, size), jnp.float32) for _ in range(levels - 1)],
            [pltpu.VMEM((rows, tail + size), jnp.float32) for _ in range(levels - 1)],
            [pltpu.VMEM((rows, size), jnp.int16) for _ in range(levels)],
            [pltpu.VMEM((rows, size), jnp.int16) for _ in range(levels)],
            pltpu.VMEM((levels, PACKED, LANES), jnp.int16),
            pltpu.VMEM((levels, PACKED, LANES), jnp.int16),
            pltpu.SemaphoreType.DMA((levels + 1,)),
            pltpu.SemaphoreType.DMA((levels + 1,)),
            pltpu.SemaphoreType.DMA((levels,)),
            pltpu.SemaphoreType.DMA((levels,)),
        ]
    return pl.pallas_call(
        functools.partial(sweep_kernel, plan, rim),
        name="sweep",
        out_shape=(
            jax.ShapeDtypeStruct((box_widths.shape[0], rows, samples), jnp.float32),
            jax.ShapeDtypeStruct((rows, LANES), jnp.float32),
            jax.ShapeDtypeStruct((box_widths.shape[0], LANES), jnp.int32),
        ),
        in_specs=[pl.BlockSpec(memory_space=pltpu.HBM)] * 6,
        out_specs=(vmem, vmem, vmem),
        scratch_shapes=[
            pltpu.VMEM((rows, widths[-1]), jnp.float32),
            pltpu.VMEM((2 * LANES, box_widths.shape[0] * LANES), jnp.bfloat16),
            pltpu.VMEM(delays.shape, jnp.int32),
            pltpu.VMEM(lower_rows.shape, jnp.int32),
            pltpu.VMEM(upper_rows.shape, jnp.int32),
            pltpu.VMEM(level_shifts.shape, jnp.int32),
            pltpu.VMEM((1, box_widths.shape[0]), jnp.int32),
            pltpu.VMEM((channels, LANES + total), jnp.bfloat16),
            pltpu.VMEM((channels, min(rim, samples)), jnp.bfloat16),
            pltpu.VMEM((COARSE * rows, FINE * channels), jnp.bfloat16),
            pltpu.VMEM((FINE * channels, TILES[0]), jnp.bfloat16),
            pltpu.VMEM((COARSE * rows, total), jnp.float32),
            [pltpu.VMEM((rows, width), jnp.float32) for _ in range(levels)],
            [pltpu.VMEM((rows, width), jnp.float32) for _ in range(levels)],
            [pltpu.VMEM((rows, tail + width), jnp.float32) for _ in range(levels)],
            coded(),
            coded(),
            scales,
            scales,
            pltpu.VMEM((rows, LANES), jnp.float32),
            pltpu.VMEM((rows, LANES), jnp.float32),
            pltpu.SemaphoreType.DMA,
            pltpu.SemaphoreType.DMA((5,)),
            pltpu.SemaphoreType.DMA((2,)),
            pltpu.SemaphoreType.DMA((2,)),
            pltpu.SemaphoreType.DMA((levels, chunks)),
            pltpu.SemaphoreType.DMA((levels, chunks)),
            pltpu.SemaphoreType.DMA((levels, chunks)),
            pltpu.SemaphoreType.DMA((levels, chunks)),
            *far,
        ],
        compiler_params=pltpu.CompilerParams(
            collective_id=0, has_side_effects=True, vmem_limit_bytes=48 * 2**20
        ),
    )(
        *[
            pltpu.with_memory_space_constraint(each, pltpu.HBM)
            for each in (filterbank, delays, lower_rows, upper_rows, level_shifts, box_widths[None])
        ]
    )


def scale_kernel(times, widths_ref, squares_ref, boxes_ref, out_ref):
    which = pl.program_id(0)
    root = jnp.sqrt(widths_ref[pl.ds(which, 1), :].astype(jnp.float32))
    factor = lax.rsqrt(squares_ref[...] / times + 1e-05) / root
    for begin in range(0, out_ref.shape[2], LANES):
        out_ref[0, :, begin : begin + LANES] = (
            boxes_ref[which, :, begin : begin + LANES] * factor
        )


def scale(widths, squares, boxes, times):
    count, rows, samples = boxes.shape
    vmem = pl.BlockSpec(memory_space=pltpu.VMEM)
    return pl.pallas_call(
        functools.partial(scale_kernel, times),
        name="scale",
        grid=(count,),
        out_shape=jax.ShapeDtypeStruct(boxes.shape, jnp.float32),
        in_specs=[vmem, vmem, vmem],
        out_specs=pl.BlockSpec((1, rows, samples), lambda i: (i, 0, 0)),
        compiler_params=pltpu.CompilerParams(vmem_limit_bytes=16 * 2**20),
    )(widths, squares, boxes)


def local(filterbank, local_delays, lower_rows, upper_rows, level_shifts, box_widths):
    samples = filterbank.shape[1]
    levels = lax.axis_size("chan").bit_length() - 1
    needs = [LANES]
    for level in reversed(range(levels)):
        needs.insert(0, needs[0] - (level == levels - 1) + DLOC * 2**level // 2 - 1)
    widths = [samples + lane_up(need + 1) for need in needs[:-1]] + [samples + LANES]
    boxes, squares, spans = sweep(
        filterbank, local_delays.T, lower_rows, upper_rows, level_shifts, box_widths, widths
    )
    return scale(spans, squares, boxes, samples * lax.axis_size("tm"))


def solution(mesh):
    placed = (
        P(("beam", "chan"), "tm"),
        P("chan", None),
        P(None, "chan"),
        P(None, "chan"),
        P(None, "chan"),
        P(),
    )
    return jax.shard_map(
        local,
        mesh=mesh,
        in_specs=placed,
        out_specs=P(None, ("beam", "chan"), "tm"),
        check_vma=False,
    )
```

```python
import functools

import jax
import jax.numpy as jnp
from jax import lax
from jax.experimental import pallas as pl
from jax.experimental.pallas import tpu as pltpu
from jax.sharding import PartitionSpec as P

DLOC = 64
LANES = 128
FINE = 8
COARSE = DLOC // FINE
CHUNKS = 3
PACKED = 16
TILES = (1024, 896, 768, 640, 512, 384, 256, 128)
EARLY = 7
FIRST = 4
SECOND = 4
STEPS = [
    ("sum", 0),
    ("meet",),
    ("send", 0),
    ("sum", 2, True),
    ("send", 2),
    ("rim",),
    ("share",),
    ("cross",),
    ("send", 1),
    ("merge", 0, 0),
    ("sum", 3, True),
    ("send", 3),
    ("merge", 0, 2),
    ("merge", 0, 1),
    ("merge", 1, 0),
    ("relay",),
    ("merge", 0, 3),
    ("merge", 1, 2),
    ("merge", 1, 1),
    ("far", 0),
    ("merge", 1, 3),
    ("merge", 2, 0),
    ("merge", 2, 2),
    ("far", 1),
    ("merge", 2, 3),
    ("merge", 2, 1),
]
MESH = pl.DeviceIdType.MESH


def lane_up(count):
    return -(-count // LANES) * LANES


def code_rows(rows):
    largest = jnp.maximum(jnp.max(jnp.abs(rows), axis=1, keepdims=True), 2.0**-100)
    exponent = jnp.floor(jnp.log2(largest))
    coded = jnp.round(jnp.clip(rows * jnp.exp2(14.0 - exponent), -32767.0, 32767.0))
    at = lax.broadcasted_iota(jnp.int32, (rows.shape[0], LANES), 0)
    to = lax.broadcasted_iota(jnp.int32, (rows.shape[0], LANES), 1)
    along = jnp.sum(jnp.where(at == to, exponent, 0.0), axis=0, keepdims=True)
    along = jnp.broadcast_to(along, (PACKED, LANES))
    return coded.astype(jnp.int32).astype(jnp.int16), along.astype(jnp.int32).astype(jnp.int16)


def decode_rows(coded, along):
    values = coded.astype(jnp.int32).astype(jnp.float32)
    exponents = along.astype(jnp.int32)[:1, : coded.shape[0]]
    return values * jnp.exp2(as_column(exponents).astype(jnp.float32) - 14.0)


def as_column(row):
    count = row.shape[1]
    at = lax.broadcasted_iota(jnp.int32, (count, count), 0)
    to = lax.broadcasted_iota(jnp.int32, (count, count), 1)
    spread = jnp.where(at == to, row.astype(jnp.float32), 0.0)
    return jnp.sum(spread, axis=1, keepdims=True).astype(jnp.int32)


def split(source):
    high = source.astype(jnp.bfloat16)
    low = (source - high.astype(jnp.float32)).astype(jnp.bfloat16)
    return high, low


def choose(lower, upper, upper_side):
    rows = lower.shape[0]
    at = lax.broadcasted_iota(jnp.int32, (rows, 2 * rows), 1)
    at = jnp.where(at >= rows, at - rows, at)
    low = jnp.where(at == lower, 1.0, 0.0)
    high = jnp.where(at == upper, 1.0, 0.0)
    none = jnp.zeros_like(low)
    own_low = jnp.where(upper_side, none, low)
    own_high = jnp.where(upper_side, high, none)
    chosen = jnp.concatenate(
        [
            jnp.concatenate([own_low, low - own_low], axis=1),
            jnp.concatenate([own_high, high - own_high], axis=1),
        ],
        axis=0,
    )
    return chosen.astype(jnp.bfloat16)


def pick(chosen, own, partner):
    stacked = jnp.concatenate([*split(own), *split(partner)], axis=0)
    return jnp.dot(chosen, stacked, preferred_element_type=jnp.float32)


def delayed(moved, shifts, reach, room):
    for bit in range(LANES.bit_length() - 1, (reach - 1).bit_length()):
        moved = jnp.where((shifts >> bit) & 1 == 1, pltpu.roll(moved, 2**bit, 1), moved)
    fine = shifts & (LANES - 1)
    lane = lax.broadcasted_iota(jnp.int32, (moved.shape[0], LANES), 1)
    index = (lane - fine) & (LANES - 1)
    early = lane < fine
    turned = [
        jnp.take_along_axis(
            moved[:, begin : begin + LANES], index, axis=1, mode="promise_in_bounds"
        )
        for begin in range(room - LANES, moved.shape[1], LANES)
    ]
    return jnp.concatenate(
        [jnp.where(early, before, now) for before, now in zip(turned, turned[1:])], axis=1
    )


def reach_of(level):
    return DLOC * 2**level // 2


class Plan:
    def __init__(self, widths, samples):
        tiles = [each // LANES for each in widths]
        self.levels = levels = len(widths) - 1
        self.width = widths[0]
        self.old = widths[0] - samples
        self.starts = starts = [tiles[0] - each for each in tiles]
        past = [sum(reach_of(each) - 1 for each in range(level)) for level in range(levels + 1)]
        if levels == 3 and samples // LANES >= 16:
            self.shared = True
            first = EARLY
            valid = [first + -(-each // LANES) for each in past]
            begins = [
                (valid[levels] * LANES - past[levels] + past[level]) // LANES
                for level in range(levels + 1)
            ]
            after = first + FIRST
            last = after + SECOND
            spans = [
                [
                    (begins[level], after),
                    (starts[level], valid[level]),
                    (after, last),
                    (last, tiles[0]),
                ]
                for level in range(levels + 1)
            ]
            self.far = (0, begins[levels - 1])
            self.steps = STEPS
        else:
            self.shared = False
            fair = (tiles[0] - 1) // CHUNKS
            most = (tiles[-1] - 1) // max(CHUNKS - 1, 1)
            later = min(fair, most) // 2 * 2 or 1
            sizes = [tiles[0] - later * (CHUNKS - 1)] + [later] * (CHUNKS - 1)
            edges = [sum(sizes[:count]) for count in range(CHUNKS + 1)]
            spans = [
                [(max(edges[c], start), edges[c + 1]) for c in range(CHUNKS)] for start in starts
            ]
            self.far = (0, 0)
            self.steps = [("meet",), ("rim",)]
            for turn in range(CHUNKS + levels):
                if turn < CHUNKS:
                    self.steps += [("sum", turn), ("send", turn)]
                self.steps += [
                    ("merge", level, turn - 1 - level)
                    for level in range(levels)
                    if 0 <= turn - 1 - level < CHUNKS
                ]
        self.spans = [[(LANES * b, LANES * e) for b, e in row] for row in spans]
        self.far = tuple(LANES * each for each in self.far)
        self.chunks = len(self.spans[0])

    def size(self, level, chunk):
        begin, end = self.spans[level][chunk]
        return end - begin

    def sends(self, level, chunk):
        return not (self.shared and level == self.levels - 1 and chunk == 1)


def sweep_kernel(
    plan,
    rim,
    fb_ref,
    delays_hbm,
    lower_hbm,
    upper_hbm,
    shifts_hbm,
    widths_hbm,
    boxes_ref,
    squares_ref,
    widths_ref,
    state,
    masks,
    delays_ref,
    lower_ref,
    upper_ref,
    shifts_ref,
    widths_row,
    ext,
    rim_in,
    onehot,
    spread,
    partial,
    owns,
    parts,
    picked,
    outgoing,
    incoming,
    scale_out,
    scale_in,
    square_out,
    square_in,
    local_sem,
    small_sem,
    pair_send,
    pair_recv,
    send_sem,
    recv_sem,
    scale_send,
    scale_recv,
    *far,
):
    channels, samples = fb_ref.shape
    rows = delays_ref.shape[0]
    levels, chunks, spans, width = plan.levels, plan.chunks, plan.spans, plan.width
    top = levels - 1
    total = rim + samples
    skip = total - width
    tail = picked[0].shape[1] - width
    sent_rim = min(rim, samples)
    empty = LANES + rim - sent_rim

    chan = lax.axis_index("chan")
    tm = lax.axis_index("tm")
    sides = [lax.rem(lax.div(chan, 1 << level), 2) for level in range(levels)]
    partners = [
        {"chan": chan + (1 << level) - (2 << level) * sides[level]} for level in range(levels)
    ]
    pair = {"tm": 1 - tm}

    barrier = pltpu.get_barrier_semaphore()
    for device in [pair] + partners:
        pl.semaphore_signal(barrier, inc=1, device_id=device, device_id_type=MESH)
    own_copy = pltpu.make_async_copy(fb_ref, ext.at[:, pl.ds(LANES + rim, samples)], local_sem)
    small_copies = [
        pltpu.make_async_copy(source, target, small_sem.at[at])
        for at, (source, target) in enumerate(
            [
                (delays_hbm, delays_ref),
                (lower_hbm, lower_ref),
                (upper_hbm, upper_ref),
                (shifts_hbm, shifts_ref),
                (widths_hbm, widths_row),
            ]
        )
    ]
    for copy in small_copies:
        copy.start()
    own_copy.start()

    def remote(source, target, sent, received, device):
        return pltpu.make_async_remote_copy(
            src_ref=source,
            dst_ref=target,
            send_sem=sent,
            recv_sem=received,
            device_id=device,
            device_id_type=MESH,
        )

    rim_copy = remote(
        fb_ref.at[:, pl.ds(samples - sent_rim, sent_rim)],
        rim_in,
        pair_send.at[0],
        pair_recv.at[0],
        pair,
    )

    ext[:, : LANES + rim] = jnp.zeros((channels, LANES + rim), jnp.bfloat16)
    for level in range(levels):
        picked[level][:, :tail] = jnp.zeros((rows, tail), jnp.float32)
        begin = tail + spans[level][0][0]
        if begin > tail:
            picked[level][:, begin - tail : begin] = jnp.zeros((rows, tail), jnp.float32)
    for copy in small_copies:
        copy.wait()
    spans_now = jnp.broadcast_to(as_column(widths_row[...]), widths_ref.shape)
    widths_ref[...] = spans_now
    at = lax.broadcasted_iota(jnp.int32, (2 * LANES, LANES), 0) - LANES
    to = lax.broadcasted_iota(jnp.int32, (2 * LANES, LANES), 1)
    for which in range(widths_ref.shape[0]):
        inside = (at <= to) & (at > to - spans_now[which : which + 1, :])
        masks[:, which * LANES : (which + 1) * LANES] = jnp.where(inside, 1.0, 0.0).astype(
            jnp.bfloat16
        )
    for coarse in range(COARSE):
        relative = delays_ref[...] - FINE * coarse
        for fine in range(FINE):
            onehot[coarse * rows : (coarse + 1) * rows, fine * channels : (fine + 1) * channels] = (
                jnp.where(relative == fine, 1.0, 0.0).astype(jnp.bfloat16)
            )

    def column_of(ref, level):
        return as_column(ref[level : level + 1, :])

    chosen = [
        choose(column_of(lower_ref, level), column_of(upper_ref, level), sides[level] == 1)
        for level in range(levels)
    ]
    shifts = [column_of(shifts_ref, level) for level in range(levels)]

    def history(level, chunk):
        begin, end = spans[level][chunk]
        return min(max(plan.old - begin, 0), end - begin)

    def exchange(level, chunk, act):
        if not plan.sends(level, chunk):
            return
        old = history(level, chunk)
        size = plan.size(level, chunk)

        def columns(begin):
            act(
                remote(
                    outgoing[level][chunk].at[:, pl.ds(begin, size - begin)],
                    incoming[level][chunk].at[:, pl.ds(begin, size - begin)],
                    send_sem.at[level, chunk],
                    recv_sem.at[level, chunk],
                    partners[level],
                )
            )

        act(
            remote(
                scale_out.at[level, chunk],
                scale_in.at[level, chunk],
                scale_send.at[level, chunk],
                scale_recv.at[level, chunk],
                partners[level],
            )
        )
        if old:
            pl.when(tm > 0)(lambda: columns(0))
            if old < size:
                pl.when(tm == 0)(lambda: columns(old))
        else:
            columns(0)

    def start(copy):
        copy.start()

    def hand_on(level, chunk, values):
        begin, end = spans[level][chunk]
        owns[level][:, begin:end] = values
        if plan.sends(level, chunk):
            outgoing[level][chunk][...], scale_out[level, chunk] = code_rows(values)

    @pl.when(tm == 0)
    def _():
        for level in range(levels):
            for chunk in range(chunks):
                old = history(level, chunk)
                if old and plan.sends(level, chunk):
                    incoming[level][chunk][:, :old] = jnp.zeros((rows, old), jnp.int16)

    def dedisperse(begin, end, known):
        first = skip + begin - (0 if known else LANES)
        tile = next(t for t in TILES if (skip + end - first) % t == 0)

        def step(index, carry):
            start = pl.multiple_of(first + index * tile, LANES)
            window = ext[:, pl.ds(start, tile + LANES)]
            for fine in range(FINE):
                spread[fine * channels : (fine + 1) * channels, :tile] = window[
                    :, LANES - fine : LANES - fine + tile
                ]
            partial[:, pl.ds(start, tile)] = jnp.dot(
                onehot[...], spread[:, :tile], preferred_element_type=jnp.float32
            )
            return carry

        lax.fori_loop(0, (skip + end - first) // tile, step, 0)
        summed = None
        for coarse in range(COARSE):
            back = skip - FINE * coarse
            term = partial[coarse * rows : (coarse + 1) * rows, back + begin : back + end]
            summed = term if summed is None else summed + term
        return summed

    def merge(level, chunk):
        begin, end = spans[level][chunk]
        after, close = spans[level + 1][chunk]
        if plan.sends(level, chunk):
            exchange(level, chunk, lambda copy: copy.wait_recv())
            parts[level][:, begin:end] = decode_rows(
                incoming[level][chunk][...], scale_in[level, chunk]
            )
        begin = min(begin, after)
        both = pick(chosen[level], owns[level][:, begin:close], parts[level][:, begin:close])
        picked[level][:, tail + begin : tail + close] = both[rows:]
        room = lane_up(reach_of(level))
        moved = picked[level][:, tail + after - room : tail + close]
        return both[:rows, after - begin :] + delayed(moved, shifts[level], reach_of(level), room)

    if plan.shared:
        (
            tables_out,
            tables_in,
            far_owns,
            far_parts,
            far_picked,
            far_coded,
            far_incoming,
            far_scale_out,
            far_scale_in,
            far_send,
            far_recv,
            far_scale_send,
            far_scale_recv,
        ) = far
        far_end = plan.far[1]

        @pl.when(tm == 0)
        def _():
            for step in range(top + 1):
                far_incoming[step][:, : plan.old] = jnp.zeros((rows, plan.old), jnp.int16)

        for level in range(top):
            far_picked[level][:, :tail] = jnp.zeros((rows, tail), jnp.float32)
            tables_out[3 * level : 3 * level + 1, :] = lower_ref[level : level + 1, :]
            tables_out[3 * level + 1 : 3 * level + 2, :] = upper_ref[level : level + 1, :]
            tables_out[3 * level + 2 : 3 * level + 3, :] = shifts_ref[level : level + 1, :]

    def far_exchange(step, act):
        device = partners[top] if step == 0 else partners[step - 1]
        source = far_incoming[0] if step == 1 else far_coded[step]
        scales = far_scale_in.at[0] if step == 1 else far_scale_out.at[step]

        def columns(begin):
            act(
                remote(
                    source.at[:, pl.ds(begin, far_end - begin)],
                    far_incoming[step].at[:, pl.ds(begin, far_end - begin)],
                    far_send.at[step],
                    far_recv.at[step],
                    device,
                )
            )

        act(
            remote(
                scales,
                far_scale_in.at[step],
                far_scale_send.at[step],
                far_scale_recv.at[step],
                device,
            )
        )
        pl.when(tm > 0)(lambda: columns(0))
        pl.when(tm == 0)(lambda: columns(plan.old))
        if step == 0:
            act(
                remote(
                    tables_out, tables_in, far_send.at[top + 1], far_recv.at[top + 1], device
                )
            )

    def far_wait(step):
        far_exchange(step, lambda copy: copy.wait_recv())
        return decode_rows(far_incoming[step][...], far_scale_in[step])

    def far_merge(level):
        far_parts[level][...] = far_wait(level + 1)
        lower, upper, later = (
            as_column(tables_in[3 * level + at : 3 * level + at + 1, :]) for at in range(3)
        )
        both = pick(
            choose(lower, upper, sides[level] == 1), far_owns[level][...], far_parts[level][...]
        )
        far_picked[level][:, tail:] = both[rows:]
        room = lane_up(reach_of(level))
        moved = far_picked[level][:, tail - room :]
        return both[:rows] + delayed(moved, later, reach_of(level), room)

    halo = plan.old // LANES
    offset = plan.starts[levels]

    def boxes(tiles):
        high, low = split(
            jnp.concatenate(
                [
                    state[:, LANES * (tile - 1 - offset) : LANES * (tile + 1 - offset)]
                    for tile in tiles
                ],
                axis=0,
            )
        )
        count = len(tiles) * rows
        for which in range(0, widths_ref.shape[0], 2):
            both = jnp.dot(
                jnp.concatenate([high, low], axis=0),
                masks[:, which * LANES : (which + 2) * LANES],
                preferred_element_type=jnp.float32,
            )
            summed = both[:count] + both[count:]
            for at, tile in enumerate(tiles):
                for each in range(2):
                    boxes_ref[which + each, :, LANES * (tile - halo) : LANES * (tile + 1 - halo)] = (
                        summed[at * rows : (at + 1) * rows, each * LANES : (each + 1) * LANES]
                    )

    def send_squares():
        square_out[...] = jnp.broadcast_to(squares, (rows, LANES))
        square_copy.start()

    square_copy = remote(square_out, square_in, pair_send.at[1], pair_recv.at[1], pair)
    finished, shown = set(), set()
    end_of_all = state.shape[1]
    own_copy.wait()
    squares = jnp.zeros((rows, 1), jnp.float32)
    for step in plan.steps:
        kind = step[0]
        if kind == "meet":
            pl.semaphore_wait(barrier, levels + 1)
            rim_copy.start()
        elif kind == "rim":
            rim_copy.wait()
            ext[:, empty : LANES + rim] = jnp.where(
                tm == 0, jnp.zeros((channels, sent_rim), jnp.bfloat16), rim_in[...]
            )
        elif kind == "sum":
            begin, end = spans[0][step[1]]
            known = len(step) > 2 or begin + skip < LANES
            hand_on(0, step[1], dedisperse(begin, end, known))
        elif kind == "send":
            exchange(0, step[1], start)
        elif kind == "share":
            begin, end = spans[0][1]
            owns[0][:, begin:end] = dedisperse(begin, end, False)
            coded, scales = code_rows(owns[0][:, :far_end])
            far_coded[0][...], far_scale_out[0] = coded, scales
            outgoing[0][1][...], scale_out[0, 1] = coded[:, begin:end], scales
        elif kind == "cross":
            far_exchange(0, start)
        elif kind == "relay":
            far_owns[0][...] = far_wait(0)
            far_exchange(1, start)
        elif kind == "far":
            level = step[1]
            values = far_merge(level)
            if level < top - 1:
                far_owns[level + 1][...] = values
                far_coded[level + 2][...], far_scale_out[level + 2] = code_rows(values)
                far_exchange(level + 2, start)
            else:
                parts[top][:, :far_end] = values
        else:
            _, level, chunk = step
            merged = merge(level, chunk)
            begin, end = spans[level + 1][chunk]
            if level < top:
                hand_on(level + 1, chunk, merged)
                exchange(level + 1, chunk, start)
            else:
                state[:, begin - LANES * offset : end - LANES * offset] = merged
                if end > plan.old:
                    fresh = merged[:, max(plan.old - begin, 0) :]
                    squares = squares + jnp.sum(fresh * fresh, axis=1, keepdims=True)
                finished |= set(range(begin // LANES, end // LANES))
                if len(finished) * LANES == end_of_all:
                    send_squares()
                ready = sorted(
                    tile
                    for tile in finished - shown
                    if tile >= halo and tile - 1 in finished
                )
                shown |= set(ready)
                for at in range(0, len(ready), 4):
                    boxes(ready[at : at + 4])
    for level in range(levels):
        for chunk in range(chunks):
            exchange(level, chunk, lambda copy: copy.wait_send())
    if plan.shared:
        for step in range(top + 1):
            far_exchange(step, lambda copy: copy.wait_send())
    square_copy.wait()
    squares_ref[...] = square_out[...] + square_in[...]


def sweep(filterbank, delays, lower_rows, upper_rows, level_shifts, box_widths, widths):
    channels, samples = filterbank.shape
    rows = delays.shape[0]
    plan = Plan(widths, samples)
    levels, chunks, width = plan.levels, plan.chunks, plan.width
    rim = lane_up(width - samples + DLOC - 1)
    total = rim + samples

    def coded():
        return [
            [pltpu.VMEM((rows, plan.size(j, c)), jnp.int16) for c in range(chunks)]
            for j in range(levels)
        ]

    tail = lane_up(reach_of(levels - 1))
    scales = pltpu.VMEM((levels, chunks, PACKED, LANES), jnp.int16)
    vmem = pl.BlockSpec(memory_space=pltpu.VMEM)
    far = []
    if plan.shared:
        size = plan.far[1] - plan.far[0]
        far = [
            pltpu.VMEM((3 * (levels - 1), rows), jnp.int32),
            pltpu.VMEM((3 * (levels - 1), rows), jnp.int32),
            [pltpu.VMEM((rows, size), jnp.float32) for _ in range(levels - 1)],
            [pltpu.VMEM((rows, size), jnp.float32) for _ in range(levels - 1)],
            [pltpu.VMEM((rows, tail + size), jnp.float32) for _ in range(levels - 1)],
            [pltpu.VMEM((rows, size), jnp.int16) for _ in range(levels)],
            [pltpu.VMEM((rows, size), jnp.int16) for _ in range(levels)],
            pltpu.VMEM((levels, PACKED, LANES), jnp.int16),
            pltpu.VMEM((levels, PACKED, LANES), jnp.int16),
            pltpu.SemaphoreType.DMA((levels + 1,)),
            pltpu.SemaphoreType.DMA((levels + 1,)),
            pltpu.SemaphoreType.DMA((levels,)),
            pltpu.SemaphoreType.DMA((levels,)),
        ]
    return pl.pallas_call(
        functools.partial(sweep_kernel, plan, rim),
        name="sweep",
        out_shape=(
            jax.ShapeDtypeStruct((box_widths.shape[0], rows, samples), jnp.float32),
            jax.ShapeDtypeStruct((rows, LANES), jnp.float32),
            jax.ShapeDtypeStruct((box_widths.shape[0], LANES), jnp.int32),
        ),
        in_specs=[pl.BlockSpec(memory_space=pltpu.HBM)] * 6,
        out_specs=(vmem, vmem, vmem),
        scratch_shapes=[
            pltpu.VMEM((rows, widths[-1]), jnp.float32),
            pltpu.VMEM((2 * LANES, box_widths.shape[0] * LANES), jnp.bfloat16),
            pltpu.VMEM(delays.shape, jnp.int32),
            pltpu.VMEM(lower_rows.shape, jnp.int32),
            pltpu.VMEM(upper_rows.shape, jnp.int32),
            pltpu.VMEM(level_shifts.shape, jnp.int32),
            pltpu.VMEM((1, box_widths.shape[0]), jnp.int32),
            pltpu.VMEM((channels, LANES + total), jnp.bfloat16),
            pltpu.VMEM((channels, min(rim, samples)), jnp.bfloat16),
            pltpu.VMEM((COARSE * rows, FINE * channels), jnp.bfloat16),
            pltpu.VMEM((FINE * channels, TILES[0]), jnp.bfloat16),
            pltpu.VMEM((COARSE * rows, total), jnp.float32),
            [pltpu.VMEM((rows, width), jnp.float32) for _ in range(levels)],
            [pltpu.VMEM((rows, width), jnp.float32) for _ in range(levels)],
            [pltpu.VMEM((rows, tail + width), jnp.float32) for _ in range(levels)],
            coded(),
            coded(),
            scales,
            scales,
            pltpu.VMEM((rows, LANES), jnp.float32),
            pltpu.VMEM((rows, LANES), jnp.float32),
            pltpu.SemaphoreType.DMA,
            pltpu.SemaphoreType.DMA((5,)),
            pltpu.SemaphoreType.DMA((2,)),
            pltpu.SemaphoreType.DMA((2,)),
            pltpu.SemaphoreType.DMA((levels, chunks)),
            pltpu.SemaphoreType.DMA((levels, chunks)),
            pltpu.SemaphoreType.DMA((levels, chunks)),
            pltpu.SemaphoreType.DMA((levels, chunks)),
            *far,
        ],
        compiler_params=pltpu.CompilerParams(
            collective_id=0, has_side_effects=True, vmem_limit_bytes=48 * 2**20
        ),
    )(
        *[
            pltpu.with_memory_space_constraint(each, pltpu.HBM)
            for each in (filterbank, delays, lower_rows, upper_rows, level_shifts, box_widths[None])
        ]
    )


def scale_kernel(times, widths_ref, squares_ref, boxes_ref, out_ref, scaled, sem):
    inverse = lax.rsqrt(squares_ref[...] / times + 1e-05)
    copies = []
    for which in range(out_ref.shape[0]):
        root = jnp.sqrt(widths_ref[which : which + 1, :].astype(jnp.float32))
        factor = inverse / root
        for begin in range(0, out_ref.shape[2], LANES):
            scaled[which, :, begin : begin + LANES] = (
                boxes_ref[which, :, begin : begin + LANES] * factor
            )
        copies.append(pltpu.make_async_copy(scaled.at[which], out_ref.at[which], sem.at[which]))
        copies[-1].start()
    for copy in copies:
        copy.wait()


def scale(widths, squares, boxes, times):
    vmem = pl.BlockSpec(memory_space=pltpu.VMEM)
    return pl.pallas_call(
        functools.partial(scale_kernel, times),
        name="scale",
        out_shape=jax.ShapeDtypeStruct(boxes.shape, jnp.float32),
        in_specs=[vmem, vmem, vmem],
        out_specs=pl.BlockSpec(memory_space=pl.ANY),
        scratch_shapes=[
            pltpu.VMEM(boxes.shape, jnp.float32),
            pltpu.SemaphoreType.DMA((boxes.shape[0],)),
        ],
        compiler_params=pltpu.CompilerParams(vmem_limit_bytes=16 * 2**20),
    )(widths, squares, boxes)


def local(filterbank, local_delays, lower_rows, upper_rows, level_shifts, box_widths):
    samples = filterbank.shape[1]
    levels = lax.axis_size("chan").bit_length() - 1
    needs = [LANES]
    for level in reversed(range(levels)):
        needs.insert(0, needs[0] - (level == levels - 1) + DLOC * 2**level // 2 - 1)
    widths = [samples + lane_up(need + 1) for need in needs[:-1]] + [samples + LANES]
    boxes, squares, spans = sweep(
        filterbank, local_delays.T, lower_rows, upper_rows, level_shifts, box_widths, widths
    )
    return scale(spans, squares, boxes, samples * lax.axis_size("tm"))


def solution(mesh):
    placed = (
        P(("beam", "chan"), "tm"),
        P("chan", None),
        P(None, "chan"),
        P(None, "chan"),
        P(None, "chan"),
        P(),
    )
    return jax.shard_map(
        local,
        mesh=mesh,
        in_specs=placed,
        out_specs=P(None, ("beam", "chan"), "tm"),
        check_vma=False,
    )
```

```python
import functools

import jax
import jax.numpy as jnp
from jax import lax
from jax.experimental import pallas as pl
from jax.experimental.pallas import tpu as pltpu
from jax.sharding import PartitionSpec as P

DLOC = 64
LANES = 128
FINE = 8
COARSE = DLOC // FINE
CHUNKS = 3
PACKED = 16
TILES = (1024, 896, 768, 640, 512, 384, 256, 128)
EARLY = 6
SIZES = (3, 5)
STEPS = [
    ("sum", 0),
    ("meet",),
    ("send", 0),
    ("sum", 2, True),
    ("send", 2),
    ("rim",),
    ("share",),
    ("cross",),
    ("send", 1),
    ("merge", 0, 0),
    ("sum", 3, True),
    ("send", 3),
    ("merge", 0, 2),
    ("merge", 1, 0),
    ("merge", 0, 1),
    ("relay",),
    ("merge", 0, 3),
    ("merge", 1, 2),
    ("merge", 1, 1),
    ("far", 0),
    ("merge", 1, 3),
    ("merge", 2, 0),
    ("merge", 2, 2),
    ("far", 1),
    ("merge", 2, 1),
    ("merge", 2, 3),
]
MESH = pl.DeviceIdType.MESH


def lane_up(count):
    return -(-count // LANES) * LANES


def packed_shape(rows, columns):
    return (rows // PACKED * (columns // LANES) + 1, PACKED, LANES)


def code_rows(rows):
    largest = jnp.maximum(jnp.max(jnp.abs(rows), axis=1, keepdims=True), 2.0**-100)
    exponent = jnp.floor(jnp.log2(largest))
    coded = jnp.round(jnp.clip(rows * jnp.exp2(14.0 - exponent), -32767.0, 32767.0))
    at = lax.broadcasted_iota(jnp.int32, (rows.shape[0], LANES), 0)
    to = lax.broadcasted_iota(jnp.int32, (rows.shape[0], LANES), 1)
    along = jnp.sum(jnp.where(at == to, exponent, 0.0), axis=0, keepdims=True)
    along = jnp.broadcast_to(along, (PACKED, LANES))
    return coded.astype(jnp.int32).astype(jnp.int16), along.astype(jnp.int32).astype(jnp.int16)


def put_rows(ref, coded, along):
    groups = coded.shape[0] // PACKED
    tiles = coded.shape[1] // LANES
    for tile in range(tiles):
        for group in range(groups):
            ref[tile * groups + group] = coded[
                group * PACKED : (group + 1) * PACKED, tile * LANES : (tile + 1) * LANES
            ]
    ref[tiles * groups] = along


def decode_rows(ref, rows):
    groups = rows // PACKED
    tiles = ref.shape[0] // groups
    coded = jnp.concatenate(
        [
            jnp.concatenate([ref[tile * groups + group] for tile in range(tiles)], axis=1)
            for group in range(groups)
        ],
        axis=0,
    )
    values = coded.astype(jnp.int32).astype(jnp.float32)
    exponents = ref[tiles * groups].astype(jnp.int32)[:1, :rows]
    return values * jnp.exp2(as_column(exponents).astype(jnp.float32) - 14.0)


def as_column(row):
    count = row.shape[1]
    at = lax.broadcasted_iota(jnp.int32, (count, count), 0)
    to = lax.broadcasted_iota(jnp.int32, (count, count), 1)
    spread = jnp.where(at == to, row.astype(jnp.float32), 0.0)
    return jnp.sum(spread, axis=1, keepdims=True).astype(jnp.int32)


def split(source):
    high = source.astype(jnp.bfloat16)
    low = (source - high.astype(jnp.float32)).astype(jnp.bfloat16)
    return high, low


def choose(lower, upper, upper_side):
    rows = lower.shape[0]
    at = lax.broadcasted_iota(jnp.int32, (rows, 2 * rows), 1)
    at = jnp.where(at >= rows, at - rows, at)
    low = jnp.where(at == lower, 1.0, 0.0)
    high = jnp.where(at == upper, 1.0, 0.0)
    none = jnp.zeros_like(low)
    own_low = jnp.where(upper_side, none, low)
    own_high = jnp.where(upper_side, high, none)
    chosen = jnp.concatenate(
        [
            jnp.concatenate([own_low, low - own_low], axis=1),
            jnp.concatenate([own_high, high - own_high], axis=1),
        ],
        axis=0,
    )
    return chosen.astype(jnp.bfloat16)


def pick(chosen, own, partner):
    stacked = jnp.concatenate([*split(own), *split(partner)], axis=0)
    return jnp.dot(chosen, stacked, preferred_element_type=jnp.float32)


def delayed(moved, shifts, reach, room):
    for bit in range(LANES.bit_length() - 1, (reach - 1).bit_length()):
        moved = jnp.where((shifts >> bit) & 1 == 1, pltpu.roll(moved, 2**bit, 1), moved)
    fine = shifts & (LANES - 1)
    lane = lax.broadcasted_iota(jnp.int32, (moved.shape[0], LANES), 1)
    index = (lane - fine) & (LANES - 1)
    early = lane < fine
    turned = [
        jnp.take_along_axis(
            moved[:, begin : begin + LANES], index, axis=1, mode="promise_in_bounds"
        )
        for begin in range(room - LANES, moved.shape[1], LANES)
    ]
    return jnp.concatenate(
        [jnp.where(early, before, now) for before, now in zip(turned, turned[1:])], axis=1
    )


def reach_of(level):
    return DLOC * 2**level // 2


class Plan:
    def __init__(self, widths, samples):
        tiles = [each // LANES for each in widths]
        self.levels = levels = len(widths) - 1
        self.width = widths[0]
        self.old = widths[0] - samples
        self.starts = starts = [tiles[0] - each for each in tiles]
        past = [sum(reach_of(each) - 1 for each in range(level)) for level in range(levels + 1)]
        if levels == 3 and samples // LANES >= 16:
            self.shared = True
            first = EARLY
            valid = [first + -(-each // LANES) for each in past]
            begins = [
                (valid[levels] * LANES - past[levels] + past[level]) // LANES
                for level in range(levels + 1)
            ]
            cuts = [first + sum(SIZES[:count]) for count in range(1, len(SIZES) + 1)] + [tiles[0]]
            spans = [
                [(begins[level], cuts[0]), (starts[level], valid[level])] + list(zip(cuts, cuts[1:]))
                for level in range(levels + 1)
            ]
            self.far = (0, begins[levels - 1])
            self.steps = STEPS
        else:
            self.shared = False
            fair = (tiles[0] - 1) // CHUNKS
            most = (tiles[-1] - 1) // max(CHUNKS - 1, 1)
            later = min(fair, most) // 2 * 2 or 1
            sizes = [tiles[0] - later * (CHUNKS - 1)] + [later] * (CHUNKS - 1)
            edges = [sum(sizes[:count]) for count in range(CHUNKS + 1)]
            spans = [
                [(max(edges[c], start), edges[c + 1]) for c in range(CHUNKS)] for start in starts
            ]
            self.far = (0, 0)
            self.steps = [("meet",), ("rim",)]
            for turn in range(CHUNKS + levels):
                if turn < CHUNKS:
                    self.steps += [("sum", turn), ("send", turn)]
                self.steps += [
                    ("merge", level, turn - 1 - level)
                    for level in range(levels)
                    if 0 <= turn - 1 - level < CHUNKS
                ]
        self.spans = [[(LANES * b, LANES * e) for b, e in row] for row in spans]
        self.far = tuple(LANES * each for each in self.far)
        self.chunks = len(self.spans[0])

    def size(self, level, chunk):
        begin, end = self.spans[level][chunk]
        return end - begin

    def sends(self, level, chunk):
        return not (self.shared and level == self.levels - 1 and chunk == 1)


def sweep_kernel(
    plan,
    rim,
    fb_ref,
    delays_hbm,
    lower_hbm,
    upper_hbm,
    shifts_hbm,
    widths_hbm,
    boxes_ref,
    squares_ref,
    widths_ref,
    state,
    masks,
    delays_ref,
    lower_ref,
    upper_ref,
    shifts_ref,
    widths_row,
    ext,
    rim_in,
    onehot,
    spread,
    partial,
    owns,
    parts,
    picked,
    outgoing,
    incoming,
    square_out,
    square_in,
    local_sem,
    small_sem,
    pair_send,
    pair_recv,
    send_sem,
    recv_sem,
    *far,
):
    channels, samples = fb_ref.shape
    rows = delays_ref.shape[0]
    levels, chunks, spans, width = plan.levels, plan.chunks, plan.spans, plan.width
    top = levels - 1
    total = rim + samples
    skip = total - width
    tail = picked[0].shape[1] - width
    sent_rim = min(rim, samples)
    empty = LANES + rim - sent_rim

    chan = lax.axis_index("chan")
    tm = lax.axis_index("tm")
    sides = [lax.rem(lax.div(chan, 1 << level), 2) for level in range(levels)]
    partners = [
        {"chan": chan + (1 << level) - (2 << level) * sides[level]} for level in range(levels)
    ]
    pair = {"tm": 1 - tm}

    barrier = pltpu.get_barrier_semaphore()
    for device in [pair] + partners:
        pl.semaphore_signal(barrier, inc=1, device_id=device, device_id_type=MESH)
    own_copy = pltpu.make_async_copy(fb_ref, ext.at[:, pl.ds(LANES + rim, samples)], local_sem)
    small_copies = [
        pltpu.make_async_copy(source, target, small_sem.at[at])
        for at, (source, target) in enumerate(
            [
                (delays_hbm, delays_ref),
                (lower_hbm, lower_ref),
                (upper_hbm, upper_ref),
                (shifts_hbm, shifts_ref),
                (widths_hbm, widths_row),
            ]
        )
    ]
    for copy in small_copies:
        copy.start()
    own_copy.start()

    def remote(source, target, sent, received, device):
        return pltpu.make_async_remote_copy(
            src_ref=source,
            dst_ref=target,
            send_sem=sent,
            recv_sem=received,
            device_id=device,
            device_id_type=MESH,
        )

    rim_copy = remote(
        fb_ref.at[:, pl.ds(samples - sent_rim, sent_rim)],
        rim_in,
        pair_send.at[0],
        pair_recv.at[0],
        pair,
    )

    ext[:, : LANES + rim] = jnp.zeros((channels, LANES + rim), jnp.bfloat16)
    for level in range(levels):
        picked[level][:, :tail] = jnp.zeros((rows, tail), jnp.float32)
        begin = tail + spans[level][0][0]
        if begin > tail:
            picked[level][:, begin - tail : begin] = jnp.zeros((rows, tail), jnp.float32)
    for copy in small_copies:
        copy.wait()
    spans_now = jnp.broadcast_to(as_column(widths_row[...]), widths_ref.shape)
    widths_ref[...] = spans_now
    at = lax.broadcasted_iota(jnp.int32, (2 * LANES, LANES), 0) - LANES
    to = lax.broadcasted_iota(jnp.int32, (2 * LANES, LANES), 1)
    for which in range(widths_ref.shape[0]):
        inside = (at <= to) & (at > to - spans_now[which : which + 1, :])
        masks[:, which * LANES : (which + 1) * LANES] = jnp.where(inside, 1.0, 0.0).astype(
            jnp.bfloat16
        )
    for coarse in range(COARSE):
        relative = delays_ref[...] - FINE * coarse
        for fine in range(FINE):
            onehot[coarse * rows : (coarse + 1) * rows, fine * channels : (fine + 1) * channels] = (
                jnp.where(relative == fine, 1.0, 0.0).astype(jnp.bfloat16)
            )

    def column_of(ref, level):
        return as_column(ref[level : level + 1, :])

    chosen = [
        choose(column_of(lower_ref, level), column_of(upper_ref, level), sides[level] == 1)
        for level in range(levels)
    ]
    shifts = [column_of(shifts_ref, level) for level in range(levels)]

    def history(level, chunk):
        begin, end = spans[level][chunk]
        return min(max(plan.old - begin, 0), end - begin)

    groups = rows // PACKED

    def from_column(ref, begin):
        skipped = begin // LANES * groups
        return ref.at[pl.ds(skipped, ref.shape[0] - skipped)]

    def exchange(level, chunk, act):
        if not plan.sends(level, chunk):
            return

        def columns(begin):
            act(
                remote(
                    from_column(outgoing[level][chunk], begin),
                    from_column(incoming[level][chunk], begin),
                    send_sem.at[level, chunk],
                    recv_sem.at[level, chunk],
                    partners[level],
                )
            )

        old = history(level, chunk)
        if old:
            pl.when(tm > 0)(lambda: columns(0))
            pl.when(tm == 0)(lambda: columns(old))
        else:
            columns(0)

    def start(copy):
        copy.start()

    def hand_on(level, chunk, values):
        begin, end = spans[level][chunk]
        owns[level][:, begin:end] = values
        if plan.sends(level, chunk):
            put_rows(outgoing[level][chunk], *code_rows(values))

    @pl.when(tm == 0)
    def _():
        for level in range(levels):
            for chunk in range(chunks):
                old = history(level, chunk)
                if old and plan.sends(level, chunk):
                    blank = old // LANES * groups
                    incoming[level][chunk][:blank] = jnp.zeros(
                        (blank, PACKED, LANES), jnp.int16
                    )

    def dedisperse(begin, end, known):
        first = skip + begin - (0 if known else LANES)
        tile = next(t for t in TILES if (skip + end - first) % t == 0)

        def step(index, carry):
            start = pl.multiple_of(first + index * tile, LANES)
            window = ext[:, pl.ds(start, tile + LANES)]
            for fine in range(FINE):
                spread[fine * channels : (fine + 1) * channels, :tile] = window[
                    :, LANES - fine : LANES - fine + tile
                ]
            partial[:, pl.ds(start, tile)] = jnp.dot(
                onehot[...], spread[:, :tile], preferred_element_type=jnp.float32
            )
            return carry

        lax.fori_loop(0, (skip + end - first) // tile, step, 0)
        summed = None
        for coarse in range(COARSE):
            back = skip - FINE * coarse
            term = partial[coarse * rows : (coarse + 1) * rows, back + begin : back + end]
            summed = term if summed is None else summed + term
        return summed

    def merge(level, chunk):
        begin, end = spans[level][chunk]
        after, close = spans[level + 1][chunk]
        if plan.sends(level, chunk):
            exchange(level, chunk, lambda copy: copy.wait_recv())
            parts[level][:, begin:end] = decode_rows(incoming[level][chunk], rows)
        begin = min(begin, after)
        both = pick(chosen[level], owns[level][:, begin:close], parts[level][:, begin:close])
        picked[level][:, tail + begin : tail + close] = both[rows:]
        room = lane_up(reach_of(level))
        moved = picked[level][:, tail + after - room : tail + close]
        return both[:rows, after - begin :] + delayed(moved, shifts[level], reach_of(level), room)

    if plan.shared:
        (
            tables_out,
            tables_in,
            far_owns,
            far_parts,
            far_picked,
            far_coded,
            far_incoming,
            far_send,
            far_recv,
        ) = far
        far_end = plan.far[1]

        @pl.when(tm == 0)
        def _():
            for step in range(top + 1):
                blank = plan.old // LANES * groups
                far_incoming[step][:blank] = jnp.zeros((blank, PACKED, LANES), jnp.int16)

        for level in range(top):
            far_picked[level][:, :tail] = jnp.zeros((rows, tail), jnp.float32)
            tables_out[3 * level : 3 * level + 1, :] = lower_ref[level : level + 1, :]
            tables_out[3 * level + 1 : 3 * level + 2, :] = upper_ref[level : level + 1, :]
            tables_out[3 * level + 2 : 3 * level + 3, :] = shifts_ref[level : level + 1, :]

    def far_exchange(step, act):
        device = partners[top] if step == 0 else partners[step - 1]
        source = far_incoming[0] if step == 1 else far_coded[step]

        def columns(begin):
            act(
                remote(
                    from_column(source, begin),
                    from_column(far_incoming[step], begin),
                    far_send.at[step],
                    far_recv.at[step],
                    device,
                )
            )

        pl.when(tm > 0)(lambda: columns(0))
        pl.when(tm == 0)(lambda: columns(plan.old))
        if step == 0:
            act(
                remote(
                    tables_out, tables_in, far_send.at[top + 1], far_recv.at[top + 1], device
                )
            )

    def far_wait(step):
        far_exchange(step, lambda copy: copy.wait_recv())
        return decode_rows(far_incoming[step], rows)

    def far_merge(level):
        far_parts[level][...] = far_wait(level + 1)
        lower, upper, later = (
            as_column(tables_in[3 * level + at : 3 * level + at + 1, :]) for at in range(3)
        )
        both = pick(
            choose(lower, upper, sides[level] == 1), far_owns[level][...], far_parts[level][...]
        )
        far_picked[level][:, tail:] = both[rows:]
        room = lane_up(reach_of(level))
        moved = far_picked[level][:, tail - room :]
        return both[:rows] + delayed(moved, later, reach_of(level), room)

    halo = plan.old // LANES
    offset = plan.starts[levels]

    def boxes(tiles):
        high, low = split(
            jnp.concatenate(
                [
                    state[:, LANES * (tile - 1 - offset) : LANES * (tile + 1 - offset)]
                    for tile in tiles
                ],
                axis=0,
            )
        )
        count = len(tiles) * rows
        for which in range(0, widths_ref.shape[0], 2):
            both = jnp.dot(
                jnp.concatenate([high, low], axis=0),
                masks[:, which * LANES : (which + 2) * LANES],
                preferred_element_type=jnp.float32,
            )
            summed = both[:count] + both[count:]
            for at, tile in enumerate(tiles):
                for each in range(2):
                    boxes_ref[which + each, :, LANES * (tile - halo) : LANES * (tile + 1 - halo)] = (
                        summed[at * rows : (at + 1) * rows, each * LANES : (each + 1) * LANES]
                    )

    def send_squares():
        square_out[...] = jnp.broadcast_to(squares, (rows, LANES))
        square_copy.start()

    square_copy = remote(square_out, square_in, pair_send.at[1], pair_recv.at[1], pair)
    finished, shown = set(), set()
    end_of_all = state.shape[1]
    own_copy.wait()
    squares = jnp.zeros((rows, 1), jnp.float32)
    for step in plan.steps:
        kind = step[0]
        if kind == "meet":
            pl.semaphore_wait(barrier, levels + 1)
            rim_copy.start()
        elif kind == "rim":
            rim_copy.wait()
            ext[:, empty : LANES + rim] = jnp.where(
                tm == 0, jnp.zeros((channels, sent_rim), jnp.bfloat16), rim_in[...]
            )
        elif kind == "sum":
            begin, end = spans[0][step[1]]
            known = len(step) > 2 or begin + skip < LANES
            hand_on(0, step[1], dedisperse(begin, end, known))
        elif kind == "send":
            exchange(0, step[1], start)
        elif kind == "share":
            begin, end = spans[0][1]
            owns[0][:, begin:end] = dedisperse(begin, end, False)
            coded, scales = code_rows(owns[0][:, :far_end])
            put_rows(far_coded[0], coded, scales)
            put_rows(outgoing[0][1], coded[:, begin:end], scales)
        elif kind == "cross":
            far_exchange(0, start)
        elif kind == "relay":
            far_owns[0][...] = far_wait(0)
            far_exchange(1, start)
        elif kind == "far":
            level = step[1]
            values = far_merge(level)
            if level < top - 1:
                far_owns[level + 1][...] = values
                put_rows(far_coded[level + 2], *code_rows(values))
                far_exchange(level + 2, start)
            else:
                parts[top][:, :far_end] = values
        else:
            _, level, chunk = step
            merged = merge(level, chunk)
            begin, end = spans[level + 1][chunk]
            if level < top:
                hand_on(level + 1, chunk, merged)
                exchange(level + 1, chunk, start)
            else:
                state[:, begin - LANES * offset : end - LANES * offset] = merged
                if end > plan.old:
                    fresh = merged[:, max(plan.old - begin, 0) :]
                    squares = squares + jnp.sum(fresh * fresh, axis=1, keepdims=True)
                finished |= set(range(begin // LANES, end // LANES))
                if len(finished) * LANES == end_of_all:
                    send_squares()
                ready = sorted(
                    tile
                    for tile in finished - shown
                    if tile >= halo and tile - 1 in finished
                )
                shown |= set(ready)
                for at in range(0, len(ready), 4):
                    boxes(ready[at : at + 4])
    for level in range(levels):
        for chunk in range(chunks):
            exchange(level, chunk, lambda copy: copy.wait_send())
    if plan.shared:
        for step in range(top + 1):
            far_exchange(step, lambda copy: copy.wait_send())
    square_copy.wait()
    squares_ref[...] = square_out[...] + square_in[...]


def sweep(filterbank, delays, lower_rows, upper_rows, level_shifts, box_widths, widths):
    channels, samples = filterbank.shape
    rows = delays.shape[0]
    plan = Plan(widths, samples)
    levels, chunks, width = plan.levels, plan.chunks, plan.width
    rim = lane_up(width - samples + DLOC - 1)
    total = rim + samples

    def coded():
        return [
            [
                pltpu.VMEM(packed_shape(rows, plan.size(j, c)), jnp.int16)
                for c in range(chunks)
            ]
            for j in range(levels)
        ]

    tail = lane_up(reach_of(levels - 1))
    vmem = pl.BlockSpec(memory_space=pltpu.VMEM)
    far = []
    if plan.shared:
        size = plan.far[1] - plan.far[0]
        far = [
            pltpu.VMEM((3 * (levels - 1), rows), jnp.int32),
            pltpu.VMEM((3 * (levels - 1), rows), jnp.int32),
            [pltpu.VMEM((rows, size), jnp.float32) for _ in range(levels - 1)],
            [pltpu.VMEM((rows, size), jnp.float32) for _ in range(levels - 1)],
            [pltpu.VMEM((rows, tail + size), jnp.float32) for _ in range(levels - 1)],
            [pltpu.VMEM(packed_shape(rows, size), jnp.int16) for _ in range(levels)],
            [pltpu.VMEM(packed_shape(rows, size), jnp.int16) for _ in range(levels)],
            pltpu.SemaphoreType.DMA((levels + 1,)),
            pltpu.SemaphoreType.DMA((levels + 1,)),
        ]
    return pl.pallas_call(
        functools.partial(sweep_kernel, plan, rim),
        name="sweep",
        out_shape=(
            jax.ShapeDtypeStruct((box_widths.shape[0], rows, samples), jnp.float32),
            jax.ShapeDtypeStruct((rows, LANES), jnp.float32),
            jax.ShapeDtypeStruct((box_widths.shape[0], LANES), jnp.int32),
        ),
        in_specs=[pl.BlockSpec(memory_space=pltpu.HBM)] * 6,
        out_specs=(vmem, vmem, vmem),
        scratch_shapes=[
            pltpu.VMEM((rows, widths[-1]), jnp.float32),
            pltpu.VMEM((2 * LANES, box_widths.shape[0] * LANES), jnp.bfloat16),
            pltpu.VMEM(delays.shape, jnp.int32),
            pltpu.VMEM(lower_rows.shape, jnp.int32),
            pltpu.VMEM(upper_rows.shape, jnp.int32),
            pltpu.VMEM(level_shifts.shape, jnp.int32),
            pltpu.VMEM((1, box_widths.shape[0]), jnp.int32),
            pltpu.VMEM((channels, LANES + total), jnp.bfloat16),
            pltpu.VMEM((channels, min(rim, samples)), jnp.bfloat16),
            pltpu.VMEM((COARSE * rows, FINE * channels), jnp.bfloat16),
            pltpu.VMEM((FINE * channels, TILES[0]), jnp.bfloat16),
            pltpu.VMEM((COARSE * rows, total), jnp.float32),
            [pltpu.VMEM((rows, width), jnp.float32) for _ in range(levels)],
            [pltpu.VMEM((rows, width), jnp.float32) for _ in range(levels)],
            [pltpu.VMEM((rows, tail + width), jnp.float32) for _ in range(levels)],
            coded(),
            coded(),
            pltpu.VMEM((rows, LANES), jnp.float32),
            pltpu.VMEM((rows, LANES), jnp.float32),
            pltpu.SemaphoreType.DMA,
            pltpu.SemaphoreType.DMA((5,)),
            pltpu.SemaphoreType.DMA((2,)),
            pltpu.SemaphoreType.DMA((2,)),
            pltpu.SemaphoreType.DMA((levels, chunks)),
            pltpu.SemaphoreType.DMA((levels, chunks)),
            *far,
        ],
        compiler_params=pltpu.CompilerParams(
            collective_id=0, has_side_effects=True, vmem_limit_bytes=48 * 2**20
        ),
    )(
        *[
            pltpu.with_memory_space_constraint(each, pltpu.HBM)
            for each in (filterbank, delays, lower_rows, upper_rows, level_shifts, box_widths[None])
        ]
    )


def scale_kernel(times, widths_ref, squares_ref, boxes_ref, out_ref, scaled, sem):
    inverse = lax.rsqrt(squares_ref[...] / times + 1e-05)
    copies = []
    for which in range(out_ref.shape[0]):
        root = jnp.sqrt(widths_ref[which : which + 1, :].astype(jnp.float32))
        factor = inverse / root
        for begin in range(0, out_ref.shape[2], LANES):
            scaled[which, :, begin : begin + LANES] = (
                boxes_ref[which, :, begin : begin + LANES] * factor
            )
        copies.append(pltpu.make_async_copy(scaled.at[which], out_ref.at[which], sem.at[which]))
        copies[-1].start()
    for copy in copies:
        copy.wait()


def scale(widths, squares, boxes, times):
    vmem = pl.BlockSpec(memory_space=pltpu.VMEM)
    return pl.pallas_call(
        functools.partial(scale_kernel, times),
        name="scale",
        out_shape=jax.ShapeDtypeStruct(boxes.shape, jnp.float32),
        in_specs=[vmem, vmem, vmem],
        out_specs=pl.BlockSpec(memory_space=pl.ANY),
        scratch_shapes=[
            pltpu.VMEM(boxes.shape, jnp.float32),
            pltpu.SemaphoreType.DMA((boxes.shape[0],)),
        ],
        compiler_params=pltpu.CompilerParams(vmem_limit_bytes=16 * 2**20),
    )(widths, squares, boxes)


def local(filterbank, local_delays, lower_rows, upper_rows, level_shifts, box_widths):
    samples = filterbank.shape[1]
    levels = lax.axis_size("chan").bit_length() - 1
    needs = [LANES]
    for level in reversed(range(levels)):
        needs.insert(0, needs[0] - (level == levels - 1) + DLOC * 2**level // 2 - 1)
    widths = [samples + lane_up(need + 1) for need in needs[:-1]] + [samples + LANES]
    boxes, squares, spans = sweep(
        filterbank, local_delays.T, lower_rows, upper_rows, level_shifts, box_widths, widths
    )
    return scale(spans, squares, boxes, samples * lax.axis_size("tm"))


def solution(mesh):
    placed = (
        P(("beam", "chan"), "tm"),
        P("chan", None),
        P(None, "chan"),
        P(None, "chan"),
        P(None, "chan"),
        P(),
    )
    return jax.shard_map(
        local,
        mesh=mesh,
        in_specs=placed,
        out_specs=P(None, ("beam", "chan"), "tm"),
        check_vma=False,
    )
```

```python
import functools

import jax
import jax.numpy as jnp
from jax import lax
from jax.experimental import pallas as pl
from jax.experimental.pallas import tpu as pltpu
from jax.sharding import PartitionSpec as P

DLOC = 64
LANES = 128
FINE = 8
COARSE = DLOC // FINE
CHUNKS = 3
PACKED = 16
TILES = (1024, 896, 768, 640, 512, 384, 256, 128)
EARLY = 6
SIZES = (3, 5)
STEPS = [
    ("sum", 0),
    ("meet",),
    ("send", 0),
    ("sum", 2, True),
    ("send", 2),
    ("rim",),
    ("share",),
    ("cross",),
    ("send", 1),
    ("merge", 0, 0),
    ("sum", 3, True),
    ("send", 3),
    ("merge", 0, 2),
    ("merge", 1, 0),
    ("merge", 0, 1),
    ("relay",),
    ("merge", 0, 3),
    ("merge", 1, 2),
    ("merge", 1, 1),
    ("far", 0),
    ("merge", 1, 3),
    ("merge", 2, 0),
    ("merge", 2, 2),
    ("far", 1),
    ("merge", 2, 1),
    ("merge", 2, 3),
]
MESH = pl.DeviceIdType.MESH


def lane_up(count):
    return -(-count // LANES) * LANES


def packed_shape(rows, columns):
    return (rows // PACKED * (columns // LANES) + 1, PACKED, LANES)


def code_rows(rows):
    largest = jnp.maximum(jnp.max(jnp.abs(rows), axis=1, keepdims=True), 2.0**-100)
    exponent = jnp.floor(jnp.log2(largest))
    coded = jnp.round(jnp.clip(rows * jnp.exp2(14.0 - exponent), -32767.0, 32767.0))
    at = lax.broadcasted_iota(jnp.int32, (rows.shape[0], LANES), 0)
    to = lax.broadcasted_iota(jnp.int32, (rows.shape[0], LANES), 1)
    along = jnp.sum(jnp.where(at == to, exponent, 0.0), axis=0, keepdims=True)
    along = jnp.broadcast_to(along, (PACKED, LANES))
    return coded.astype(jnp.int32).astype(jnp.int16), along.astype(jnp.int32).astype(jnp.int16)


def put_rows(ref, coded, along):
    groups = coded.shape[0] // PACKED
    tiles = coded.shape[1] // LANES
    for tile in range(tiles):
        for group in range(groups):
            ref[tile * groups + group] = coded[
                group * PACKED : (group + 1) * PACKED, tile * LANES : (tile + 1) * LANES
            ]
    ref[tiles * groups] = along


def decode_rows(ref, rows):
    groups = rows // PACKED
    tiles = ref.shape[0] // groups
    coded = jnp.concatenate(
        [
            jnp.concatenate([ref[tile * groups + group] for tile in range(tiles)], axis=1)
            for group in range(groups)
        ],
        axis=0,
    )
    values = coded.astype(jnp.int32).astype(jnp.float32)
    exponents = ref[tiles * groups].astype(jnp.int32)[:1, :rows]
    return values * jnp.exp2(as_column(exponents).astype(jnp.float32) - 14.0)


def as_column(row):
    count = row.shape[1]
    at = lax.broadcasted_iota(jnp.int32, (count, count), 0)
    to = lax.broadcasted_iota(jnp.int32, (count, count), 1)
    spread = jnp.where(at == to, row.astype(jnp.float32), 0.0)
    return jnp.sum(spread, axis=1, keepdims=True).astype(jnp.int32)


def split(source):
    high = source.astype(jnp.bfloat16)
    low = (source - high.astype(jnp.float32)).astype(jnp.bfloat16)
    return high, low


def choose(lower, upper, upper_side):
    rows = lower.shape[0]
    at = lax.broadcasted_iota(jnp.int32, (rows, 2 * rows), 1)
    at = jnp.where(at >= rows, at - rows, at)
    low = jnp.where(at == lower, 1.0, 0.0)
    high = jnp.where(at == upper, 1.0, 0.0)
    none = jnp.zeros_like(low)
    own_low = jnp.where(upper_side, none, low)
    own_high = jnp.where(upper_side, high, none)
    chosen = jnp.concatenate(
        [
            jnp.concatenate([own_low, low - own_low], axis=1),
            jnp.concatenate([own_high, high - own_high], axis=1),
        ],
        axis=0,
    )
    return chosen.astype(jnp.bfloat16)


def pick(chosen, own, partner):
    stacked = jnp.concatenate([*split(own), *split(partner)], axis=0)
    return jnp.dot(chosen, stacked, preferred_element_type=jnp.float32)


def delayed(moved, shifts, reach, room):
    for bit in range(LANES.bit_length() - 1, (reach - 1).bit_length()):
        moved = jnp.where((shifts >> bit) & 1 == 1, pltpu.roll(moved, 2**bit, 1), moved)
    fine = shifts & (LANES - 1)
    lane = lax.broadcasted_iota(jnp.int32, (moved.shape[0], LANES), 1)
    index = (lane - fine) & (LANES - 1)
    early = lane < fine
    turned = [
        jnp.take_along_axis(
            moved[:, begin : begin + LANES], index, axis=1, mode="promise_in_bounds"
        )
        for begin in range(room - LANES, moved.shape[1], LANES)
    ]
    return jnp.concatenate(
        [jnp.where(early, before, now) for before, now in zip(turned, turned[1:])], axis=1
    )


def reach_of(level):
    return DLOC * 2**level // 2


class Plan:
    def __init__(self, widths, samples):
        tiles = [each // LANES for each in widths]
        self.levels = levels = len(widths) - 1
        self.width = widths[0]
        self.old = widths[0] - samples
        self.starts = starts = [tiles[0] - each for each in tiles]
        past = [sum(reach_of(each) - 1 for each in range(level)) for level in range(levels + 1)]
        if levels == 3 and samples // LANES >= 16:
            self.shared = True
            first = EARLY
            valid = [first + -(-each // LANES) for each in past]
            begins = [
                (valid[levels] * LANES - past[levels] + past[level]) // LANES
                for level in range(levels + 1)
            ]
            cuts = [first + sum(SIZES[:count]) for count in range(1, len(SIZES) + 1)] + [tiles[0]]
            spans = [
                [(begins[level], cuts[0]), (starts[level], valid[level])] + list(zip(cuts, cuts[1:]))
                for level in range(levels + 1)
            ]
            self.far = (0, begins[levels - 1])
            self.steps = STEPS
        else:
            self.shared = False
            fair = (tiles[0] - 1) // CHUNKS
            most = (tiles[-1] - 1) // max(CHUNKS - 1, 1)
            later = min(fair, most) // 2 * 2 or 1
            sizes = [tiles[0] - later * (CHUNKS - 1)] + [later] * (CHUNKS - 1)
            edges = [sum(sizes[:count]) for count in range(CHUNKS + 1)]
            spans = [
                [(max(edges[c], start), edges[c + 1]) for c in range(CHUNKS)] for start in starts
            ]
            self.far = (0, 0)
            self.steps = [("meet",), ("rim",)]
            for turn in range(CHUNKS + levels):
                if turn < CHUNKS:
                    self.steps += [("sum", turn), ("send", turn)]
                self.steps += [
                    ("merge", level, turn - 1 - level)
                    for level in range(levels)
                    if 0 <= turn - 1 - level < CHUNKS
                ]
        self.spans = [[(LANES * b, LANES * e) for b, e in row] for row in spans]
        self.far = tuple(LANES * each for each in self.far)
        self.chunks = len(self.spans[0])

    def size(self, level, chunk):
        begin, end = self.spans[level][chunk]
        return end - begin

    def sends(self, level, chunk):
        return not (self.shared and level == self.levels - 1 and chunk == 1)


def sweep_kernel(
    plan,
    rim,
    fb_ref,
    delays_hbm,
    lower_hbm,
    upper_hbm,
    shifts_hbm,
    widths_hbm,
    boxes_ref,
    squares_ref,
    widths_ref,
    state,
    masks,
    delays_ref,
    lower_ref,
    upper_ref,
    shifts_ref,
    widths_row,
    ext,
    rim_in,
    onehot,
    spread,
    partial,
    owns,
    parts,
    picked,
    outgoing,
    incoming,
    square_out,
    square_in,
    local_sem,
    small_sem,
    pair_send,
    pair_recv,
    send_sem,
    recv_sem,
    *far,
):
    channels, samples = fb_ref.shape
    rows = delays_ref.shape[0]
    levels, chunks, spans, width = plan.levels, plan.chunks, plan.spans, plan.width
    top = levels - 1
    total = rim + samples
    skip = total - width
    tail = picked[0].shape[1] - width
    sent_rim = min(rim, samples)
    empty = LANES + rim - sent_rim

    chan = lax.axis_index("chan")
    tm = lax.axis_index("tm")
    sides = [lax.rem(lax.div(chan, 1 << level), 2) for level in range(levels)]
    partners = [
        {"chan": chan + (1 << level) - (2 << level) * sides[level]} for level in range(levels)
    ]
    pair = {"tm": 1 - tm}

    barrier = pltpu.get_barrier_semaphore()
    for device in [pair] + partners:
        pl.semaphore_signal(barrier, inc=1, device_id=device, device_id_type=MESH)
    cut = spans[0][0][1] - plan.old if plan.shared else samples // 2
    own_copies = [
        pltpu.make_async_copy(
            fb_ref.at[:, pl.ds(begin, size)],
            ext.at[:, pl.ds(LANES + rim + begin, size)],
            local_sem.at[at],
        )
        for at, (begin, size) in enumerate([(0, cut), (cut, samples - cut)])
    ]
    own_copies[0].start()
    small_copies = [
        pltpu.make_async_copy(source, target, small_sem.at[at])
        for at, (source, target) in enumerate(
            [
                (delays_hbm, delays_ref),
                (lower_hbm, lower_ref),
                (upper_hbm, upper_ref),
                (shifts_hbm, shifts_ref),
                (widths_hbm, widths_row),
            ]
        )
    ]
    for copy in small_copies:
        copy.start()
    own_copies[1].start()

    def remote(source, target, sent, received, device):
        return pltpu.make_async_remote_copy(
            src_ref=source,
            dst_ref=target,
            send_sem=sent,
            recv_sem=received,
            device_id=device,
            device_id_type=MESH,
        )

    rim_copy = remote(
        fb_ref.at[:, pl.ds(samples - sent_rim, sent_rim)],
        rim_in,
        pair_send.at[0],
        pair_recv.at[0],
        pair,
    )

    ext[:, : LANES + rim] = jnp.zeros((channels, LANES + rim), jnp.bfloat16)
    for level in range(levels):
        picked[level][:, :tail] = jnp.zeros((rows, tail), jnp.float32)
        begin = tail + spans[level][0][0]
        if begin > tail:
            picked[level][:, begin - tail : begin] = jnp.zeros((rows, tail), jnp.float32)
    for copy in small_copies:
        copy.wait()
    spans_now = jnp.broadcast_to(as_column(widths_row[...]), widths_ref.shape)
    widths_ref[...] = spans_now
    at = lax.broadcasted_iota(jnp.int32, (2 * LANES, LANES), 0) - LANES
    to = lax.broadcasted_iota(jnp.int32, (2 * LANES, LANES), 1)
    for which in range(widths_ref.shape[0]):
        inside = (at <= to) & (at > to - spans_now[which : which + 1, :])
        masks[:, which * LANES : (which + 1) * LANES] = jnp.where(inside, 1.0, 0.0).astype(
            jnp.bfloat16
        )
    for coarse in range(COARSE):
        relative = delays_ref[...] - FINE * coarse
        for fine in range(FINE):
            onehot[coarse * rows : (coarse + 1) * rows, fine * channels : (fine + 1) * channels] = (
                jnp.where(relative == fine, 1.0, 0.0).astype(jnp.bfloat16)
            )

    def column_of(ref, level):
        return as_column(ref[level : level + 1, :])

    chosen = [
        choose(column_of(lower_ref, level), column_of(upper_ref, level), sides[level] == 1)
        for level in range(levels)
    ]
    shifts = [column_of(shifts_ref, level) for level in range(levels)]

    def history(level, chunk):
        begin, end = spans[level][chunk]
        return min(max(plan.old - begin, 0), end - begin)

    groups = rows // PACKED

    def from_column(ref, begin):
        skipped = begin // LANES * groups
        return ref.at[pl.ds(skipped, ref.shape[0] - skipped)]

    def exchange(level, chunk, act):
        if not plan.sends(level, chunk):
            return

        def columns(begin):
            act(
                remote(
                    from_column(outgoing[level][chunk], begin),
                    from_column(incoming[level][chunk], begin),
                    send_sem.at[level, chunk],
                    recv_sem.at[level, chunk],
                    partners[level],
                )
            )

        old = history(level, chunk)
        if old:
            pl.when(tm > 0)(lambda: columns(0))
            pl.when(tm == 0)(lambda: columns(old))
        else:
            columns(0)

    def start(copy):
        copy.start()

    def hand_on(level, chunk, values):
        begin, end = spans[level][chunk]
        owns[level][:, begin:end] = values
        if plan.sends(level, chunk):
            put_rows(outgoing[level][chunk], *code_rows(values))

    @pl.when(tm == 0)
    def _():
        for level in range(levels):
            for chunk in range(chunks):
                old = history(level, chunk)
                if old and plan.sends(level, chunk):
                    blank = old // LANES * groups
                    incoming[level][chunk][:blank] = jnp.zeros(
                        (blank, PACKED, LANES), jnp.int16
                    )

    def dedisperse(begin, end, known):
        first = skip + begin - (0 if known else LANES)
        tile = next(t for t in TILES if (skip + end - first) % t == 0)

        def step(index, carry):
            start = pl.multiple_of(first + index * tile, LANES)
            window = ext[:, pl.ds(start, tile + LANES)]
            for fine in range(FINE):
                spread[fine * channels : (fine + 1) * channels, :tile] = window[
                    :, LANES - fine : LANES - fine + tile
                ]
            partial[:, pl.ds(start, tile)] = jnp.dot(
                onehot[...], spread[:, :tile], preferred_element_type=jnp.float32
            )
            return carry

        lax.fori_loop(0, (skip + end - first) // tile, step, 0)
        summed = None
        for coarse in range(COARSE):
            back = skip - FINE * coarse
            term = partial[coarse * rows : (coarse + 1) * rows, back + begin : back + end]
            summed = term if summed is None else summed + term
        return summed

    def merge(level, chunk):
        begin, end = spans[level][chunk]
        after, close = spans[level + 1][chunk]
        if plan.sends(level, chunk):
            exchange(level, chunk, lambda copy: copy.wait_recv())
            parts[level][:, begin:end] = decode_rows(incoming[level][chunk], rows)
        begin = min(begin, after)
        both = pick(chosen[level], owns[level][:, begin:close], parts[level][:, begin:close])
        picked[level][:, tail + begin : tail + close] = both[rows:]
        room = lane_up(reach_of(level))
        moved = picked[level][:, tail + after - room : tail + close]
        return both[:rows, after - begin :] + delayed(moved, shifts[level], reach_of(level), room)

    if plan.shared:
        (
            tables_out,
            tables_in,
            far_owns,
            far_parts,
            far_picked,
            far_coded,
            far_incoming,
            far_send,
            far_recv,
        ) = far
        far_end = plan.far[1]

        @pl.when(tm == 0)
        def _():
            for step in range(top + 1):
                blank = plan.old // LANES * groups
                far_incoming[step][:blank] = jnp.zeros((blank, PACKED, LANES), jnp.int16)

        for level in range(top):
            far_picked[level][:, :tail] = jnp.zeros((rows, tail), jnp.float32)
            tables_out[3 * level : 3 * level + 1, :] = lower_ref[level : level + 1, :]
            tables_out[3 * level + 1 : 3 * level + 2, :] = upper_ref[level : level + 1, :]
            tables_out[3 * level + 2 : 3 * level + 3, :] = shifts_ref[level : level + 1, :]

    def far_exchange(step, act):
        device = partners[top] if step == 0 else partners[step - 1]
        source = far_incoming[0] if step == 1 else far_coded[step]

        def columns(begin):
            act(
                remote(
                    from_column(source, begin),
                    from_column(far_incoming[step], begin),
                    far_send.at[step],
                    far_recv.at[step],
                    device,
                )
            )

        pl.when(tm > 0)(lambda: columns(0))
        pl.when(tm == 0)(lambda: columns(plan.old))
        if step == 0:
            act(
                remote(
                    tables_out, tables_in, far_send.at[top + 1], far_recv.at[top + 1], device
                )
            )

    def far_wait(step):
        far_exchange(step, lambda copy: copy.wait_recv())
        return decode_rows(far_incoming[step], rows)

    def far_merge(level):
        far_parts[level][...] = far_wait(level + 1)
        lower, upper, later = (
            as_column(tables_in[3 * level + at : 3 * level + at + 1, :]) for at in range(3)
        )
        both = pick(
            choose(lower, upper, sides[level] == 1), far_owns[level][...], far_parts[level][...]
        )
        far_picked[level][:, tail:] = both[rows:]
        room = lane_up(reach_of(level))
        moved = far_picked[level][:, tail - room :]
        return both[:rows] + delayed(moved, later, reach_of(level), room)

    halo = plan.old // LANES
    offset = plan.starts[levels]

    def boxes(tiles):
        high, low = split(
            jnp.concatenate(
                [
                    state[:, LANES * (tile - 1 - offset) : LANES * (tile + 1 - offset)]
                    for tile in tiles
                ],
                axis=0,
            )
        )
        count = len(tiles) * rows
        for which in range(0, widths_ref.shape[0], 2):
            both = jnp.dot(
                jnp.concatenate([high, low], axis=0),
                masks[:, which * LANES : (which + 2) * LANES],
                preferred_element_type=jnp.float32,
            )
            summed = both[:count] + both[count:]
            for at, tile in enumerate(tiles):
                for each in range(2):
                    boxes_ref[which + each, :, LANES * (tile - halo) : LANES * (tile + 1 - halo)] = (
                        summed[at * rows : (at + 1) * rows, each * LANES : (each + 1) * LANES]
                    )

    def send_squares():
        square_out[...] = jnp.broadcast_to(squares, (rows, LANES))
        square_copy.start()

    square_copy = remote(square_out, square_in, pair_send.at[1], pair_recv.at[1], pair)
    finished, shown = set(), set()
    end_of_all = state.shape[1]
    own_copies[0].wait()
    if not plan.shared:
        own_copies[1].wait()
    squares = jnp.zeros((rows, 1), jnp.float32)
    for step in plan.steps:
        kind = step[0]
        if kind == "meet":
            pl.semaphore_wait(barrier, levels + 1)
            rim_copy.start()
            if plan.shared:
                own_copies[1].wait()
        elif kind == "rim":
            rim_copy.wait()
            ext[:, empty : LANES + rim] = jnp.where(
                tm == 0, jnp.zeros((channels, sent_rim), jnp.bfloat16), rim_in[...]
            )
        elif kind == "sum":
            begin, end = spans[0][step[1]]
            known = len(step) > 2 or begin + skip < LANES
            hand_on(0, step[1], dedisperse(begin, end, known))
        elif kind == "send":
            exchange(0, step[1], start)
        elif kind == "share":
            begin, end = spans[0][1]
            owns[0][:, begin:end] = dedisperse(begin, end, False)
            coded, scales = code_rows(owns[0][:, :far_end])
            put_rows(far_coded[0], coded, scales)
            put_rows(outgoing[0][1], coded[:, begin:end], scales)
        elif kind == "cross":
            far_exchange(0, start)
        elif kind == "relay":
            far_owns[0][...] = far_wait(0)
            far_exchange(1, start)
        elif kind == "far":
            level = step[1]
            values = far_merge(level)
            if level < top - 1:
                far_owns[level + 1][...] = values
                put_rows(far_coded[level + 2], *code_rows(values))
                far_exchange(level + 2, start)
            else:
                parts[top][:, :far_end] = values
        else:
            _, level, chunk = step
            merged = merge(level, chunk)
            begin, end = spans[level + 1][chunk]
            if level < top:
                hand_on(level + 1, chunk, merged)
                exchange(level + 1, chunk, start)
            else:
                state[:, begin - LANES * offset : end - LANES * offset] = merged
                if end > plan.old:
                    fresh = merged[:, max(plan.old - begin, 0) :]
                    squares = squares + jnp.sum(fresh * fresh, axis=1, keepdims=True)
                finished |= set(range(begin // LANES, end // LANES))
                if len(finished) * LANES == end_of_all:
                    send_squares()
                ready = sorted(
                    tile
                    for tile in finished - shown
                    if tile >= halo and tile - 1 in finished
                )
                shown |= set(ready)
                for at in range(0, len(ready), 4):
                    boxes(ready[at : at + 4])
    for level in range(levels):
        for chunk in range(chunks):
            exchange(level, chunk, lambda copy: copy.wait_send())
    if plan.shared:
        for step in range(top + 1):
            far_exchange(step, lambda copy: copy.wait_send())
    square_copy.wait()
    squares_ref[...] = square_out[...] + square_in[...]


def sweep(filterbank, delays, lower_rows, upper_rows, level_shifts, box_widths, widths):
    channels, samples = filterbank.shape
    rows = delays.shape[0]
    plan = Plan(widths, samples)
    levels, chunks, width = plan.levels, plan.chunks, plan.width
    rim = lane_up(width - samples + DLOC - 1)
    total = rim + samples

    def coded():
        return [
            [
                pltpu.VMEM(packed_shape(rows, plan.size(j, c)), jnp.int16)
                for c in range(chunks)
            ]
            for j in range(levels)
        ]

    tail = lane_up(reach_of(levels - 1))
    vmem = pl.BlockSpec(memory_space=pltpu.VMEM)
    far = []
    if plan.shared:
        size = plan.far[1] - plan.far[0]
        far = [
            pltpu.VMEM((3 * (levels - 1), rows), jnp.int32),
            pltpu.VMEM((3 * (levels - 1), rows), jnp.int32),
            [pltpu.VMEM((rows, size), jnp.float32) for _ in range(levels - 1)],
            [pltpu.VMEM((rows, size), jnp.float32) for _ in range(levels - 1)],
            [pltpu.VMEM((rows, tail + size), jnp.float32) for _ in range(levels - 1)],
            [pltpu.VMEM(packed_shape(rows, size), jnp.int16) for _ in range(levels)],
            [pltpu.VMEM(packed_shape(rows, size), jnp.int16) for _ in range(levels)],
            pltpu.SemaphoreType.DMA((levels + 1,)),
            pltpu.SemaphoreType.DMA((levels + 1,)),
        ]
    return pl.pallas_call(
        functools.partial(sweep_kernel, plan, rim),
        name="sweep",
        out_shape=(
            jax.ShapeDtypeStruct((box_widths.shape[0], rows, samples), jnp.float32),
            jax.ShapeDtypeStruct((rows, LANES), jnp.float32),
            jax.ShapeDtypeStruct((box_widths.shape[0], LANES), jnp.int32),
        ),
        in_specs=[pl.BlockSpec(memory_space=pltpu.HBM)] * 6,
        out_specs=(vmem, vmem, vmem),
        scratch_shapes=[
            pltpu.VMEM((rows, widths[-1]), jnp.float32),
            pltpu.VMEM((2 * LANES, box_widths.shape[0] * LANES), jnp.bfloat16),
            pltpu.VMEM(delays.shape, jnp.int32),
            pltpu.VMEM(lower_rows.shape, jnp.int32),
            pltpu.VMEM(upper_rows.shape, jnp.int32),
            pltpu.VMEM(level_shifts.shape, jnp.int32),
            pltpu.VMEM((1, box_widths.shape[0]), jnp.int32),
            pltpu.VMEM((channels, LANES + total), jnp.bfloat16),
            pltpu.VMEM((channels, min(rim, samples)), jnp.bfloat16),
            pltpu.VMEM((COARSE * rows, FINE * channels), jnp.bfloat16),
            pltpu.VMEM((FINE * channels, TILES[0]), jnp.bfloat16),
            pltpu.VMEM((COARSE * rows, total), jnp.float32),
            [pltpu.VMEM((rows, width), jnp.float32) for _ in range(levels)],
            [pltpu.VMEM((rows, width), jnp.float32) for _ in range(levels)],
            [pltpu.VMEM((rows, tail + width), jnp.float32) for _ in range(levels)],
            coded(),
            coded(),
            pltpu.VMEM((rows, LANES), jnp.float32),
            pltpu.VMEM((rows, LANES), jnp.float32),
            pltpu.SemaphoreType.DMA((2,)),
            pltpu.SemaphoreType.DMA((5,)),
            pltpu.SemaphoreType.DMA((2,)),
            pltpu.SemaphoreType.DMA((2,)),
            pltpu.SemaphoreType.DMA((levels, chunks)),
            pltpu.SemaphoreType.DMA((levels, chunks)),
            *far,
        ],
        compiler_params=pltpu.CompilerParams(
            collective_id=0, has_side_effects=True, vmem_limit_bytes=48 * 2**20
        ),
    )(
        *[
            pltpu.with_memory_space_constraint(each, pltpu.HBM)
            for each in (filterbank, delays, lower_rows, upper_rows, level_shifts, box_widths[None])
        ]
    )


def scale_kernel(times, widths_ref, squares_ref, boxes_ref, out_ref, scaled, sem):
    inverse = lax.rsqrt(squares_ref[...] / times + 1e-05)
    copies = []
    for which in range(out_ref.shape[0]):
        root = jnp.sqrt(widths_ref[which : which + 1, :].astype(jnp.float32))
        factor = inverse / root
        for begin in range(0, out_ref.shape[2], LANES):
            scaled[which, :, begin : begin + LANES] = (
                boxes_ref[which, :, begin : begin + LANES] * factor
            )
        copies.append(pltpu.make_async_copy(scaled.at[which], out_ref.at[which], sem.at[which]))
        copies[-1].start()
    for copy in copies:
        copy.wait()


def scale(widths, squares, boxes, times):
    vmem = pl.BlockSpec(memory_space=pltpu.VMEM)
    return pl.pallas_call(
        functools.partial(scale_kernel, times),
        name="scale",
        out_shape=jax.ShapeDtypeStruct(boxes.shape, jnp.float32),
        in_specs=[vmem, vmem, vmem],
        out_specs=pl.BlockSpec(memory_space=pl.ANY),
        scratch_shapes=[
            pltpu.VMEM(boxes.shape, jnp.float32),
            pltpu.SemaphoreType.DMA((boxes.shape[0],)),
        ],
        compiler_params=pltpu.CompilerParams(vmem_limit_bytes=16 * 2**20),
    )(widths, squares, boxes)


def local(filterbank, local_delays, lower_rows, upper_rows, level_shifts, box_widths):
    samples = filterbank.shape[1]
    levels = lax.axis_size("chan").bit_length() - 1
    needs = [LANES]
    for level in reversed(range(levels)):
        needs.insert(0, needs[0] - (level == levels - 1) + DLOC * 2**level // 2 - 1)
    widths = [samples + lane_up(need + 1) for need in needs[:-1]] + [samples + LANES]
    boxes, squares, spans = sweep(
        filterbank, local_delays.T, lower_rows, upper_rows, level_shifts, box_widths, widths
    )
    return scale(spans, squares, boxes, samples * lax.axis_size("tm"))


def solution(mesh):
    placed = (
        P(("beam", "chan"), "tm"),
        P("chan", None),
        P(None, "chan"),
        P(None, "chan"),
        P(None, "chan"),
        P(),
    )
    return jax.shard_map(
        local,
        mesh=mesh,
        in_specs=placed,
        out_specs=P(None, ("beam", "chan"), "tm"),
        check_vma=False,
    )
```
